32 devices in a mesh: tm: 16 (over z, y, core), head: 2 (over x).
Axes of the slice: x: 2, y: 2, z: 4, core: 2. Of those that a mesh axis runs over, the one named last changes fastest.
Arguments:
- frames: bfloat16 [32768, 1024], P('tm'), may hold values from -28 to 28
- w_query: bfloat16 [1024, 1024], P(None, 'head'), may hold values from -0.5 to 0.5
- w_key: bfloat16 [1024, 1024], P(None, 'head'), may hold values from -0.7 to 0.7
- w_value: bfloat16 [1024, 1024], P(None, 'head'), may hold values from -0.1875 to 0.1875
- w_out: bfloat16 [1024, 1024], replicated, may hold values from -0.5 to 0.5
Outputs:
- mixed: bfloat16 [32768, 1024], P('tm', 'head')
The draws below stay inside these ranges and needn't reach their ends.
All inputs are finite; a program needn't handle non-finite values.
Results may differ from the reference program's by a relative error of at most 0.013.
Values may be sent and summed in bfloat16 or wider, within the bound.
A program may use at most 128 MiB of HBM per device.

```python
import jax
import jax.numpy as jnp
from jax import lax

D = 1024
HEADS = 16
DH = 64
BLK = 2048
WIN = 512
PK = 256
LEVELS = 4
FRAMES = 32768


def shared_rows(key):
    return jnp.clip(jax.random.normal(jax.random.fold_in(key, 11), (D, D), jnp.float32), -4.0, 4.0)


def draw_w_query(key, part):
    return (shared_rows(key) * D ** (-0.5)).astype(jnp.bfloat16)


def draw_w_key(key, part):
    noise = jnp.clip(jax.random.normal(jax.random.fold_in(key, 12), (D, D), jnp.float32), -4.0, 4.0)
    return ((0.6 * shared_rows(key) + 0.8 * noise) * D ** (-0.5)).astype(jnp.bfloat16)


def draw_frames(key, part):
    slot_len = BLK // PK
    slots = FRAMES // slot_len
    blocks = FRAMES // BLK
    block_scale = jnp.exp(jax.random.uniform(jax.random.fold_in(key, 31), (blocks,), jnp.float32, -1.0, 1.0))
    frame_scale = jnp.repeat(block_scale, BLK, axis=0)
    base = jnp.clip(jax.random.normal(jax.random.fold_in(key, 26), (slots, D), jnp.float32), -4.0, 4.0)
    jitter = jnp.clip(jax.random.normal(jax.random.fold_in(key, 27), (FRAMES, D), jnp.float32), -4.0, 4.0)
    result = jnp.clip((jnp.repeat(base, slot_len, axis=0) + 0.5 * jitter) * frame_scale[:, None], -6.0, 6.0)
    return result.astype(jnp.bfloat16)


def steps_of(key, dims, pieces, low, largest):
    factor_of, own = 1.0, jax.random.fold_in(key, 6)
    for dim, blocks in pieces:
        heights = jnp.exp(jax.random.uniform(jax.random.fold_in(own, dim), (blocks,), jnp.float32, low / len(pieces), largest / len(pieces)))
        factor_of = factor_of * jnp.repeat(heights, dims[dim] // blocks).reshape([-1 if axis == dim else 1 for axis in range(len(dims))])
    return factor_of


def gaussian(own_key, extent, spread, most, shards=(), held_as=jnp.bfloat16):
    gain = steps_of(own_key, extent, shards, -0.22, 0.18) if shards else 1.0
    values = jax.random.normal(own_key, extent, jnp.float32) * spread * gain
    return jnp.minimum(jnp.maximum(values, -most), most).astype(held_as)


def setup_inputs(seed: int = 0) -> dict:
    seeds = jax.random.split(jax.random.key(seed), 6)
    frames = draw_frames(jax.random.fold_in(seeds[5], 71), 0)
    w_query = draw_w_query(jax.random.fold_in(seeds[5], 71), 0)
    w_key = draw_w_key(jax.random.fold_in(seeds[5], 71), 0)
    w_value = gaussian(seeds[3], (D, D), D ** -0.5, 0.1875, ((1, 2),))
    w_out = gaussian(seeds[4], (D, D), (D // 8) ** -0.5, 0.5)
    return dict(frames=frames, w_query=w_query, w_key=w_key, w_value=w_value, w_out=w_out)


def reference(frames, w_query, w_key, w_value, w_out):
    queries = jnp.dot(frames, w_query, preferred_element_type=jnp.float32).astype(jnp.bfloat16)
    keys = jnp.dot(frames, w_key, preferred_element_type=jnp.float32).astype(jnp.bfloat16)
    values = jnp.dot(frames, w_value, preferred_element_type=jnp.float32).astype(jnp.bfloat16)
    blocks = FRAMES // BLK
    pooled_keys = keys.astype(jnp.float32).reshape(blocks, PK, BLK // PK, D).mean(axis=2).astype(jnp.bfloat16)
    pooled_values = values.astype(jnp.float32).reshape(blocks, PK, BLK // PK, D).mean(axis=2).astype(jnp.bfloat16)
    qrows = min(512, BLK)
    scale = DH ** -0.5

    def one_block(index):
        start = index * BLK
        own_q = lax.dynamic_slice_in_dim(queries, start, BLK, 0)
        own_k = lax.dynamic_slice_in_dim(keys, start, BLK, 0)
        own_v = lax.dynamic_slice_in_dim(values, start, BLK, 0)
        rim_start = jnp.maximum(start - WIN, 0).astype(jnp.int32)
        rim_k = lax.dynamic_slice_in_dim(keys, rim_start, WIN, 0)
        rim_v = lax.dynamic_slice_in_dim(values, rim_start, WIN, 0)
        key_list = [own_k, rim_k]
        value_list = [own_v, rim_v]
        valid_list = [jnp.full((WIN,), index >= 1)]
        for level in range(LEVELS):
            dist = 2 ** level
            source = jnp.maximum(index - dist, 0).astype(jnp.int32)
            key_list.append(lax.dynamic_index_in_dim(pooled_keys, source, 0, keepdims=False))
            value_list.append(lax.dynamic_index_in_dim(pooled_values, source, 0, keepdims=False))
            valid_list.append(jnp.full((PK,), index >= dist))
        all_k = jnp.concatenate(key_list, 0).astype(jnp.float32).reshape(-1, HEADS, DH)
        all_v = jnp.concatenate(value_list, 0).astype(jnp.float32).reshape(-1, HEADS, DH)
        extra_valid = jnp.concatenate(valid_list, 0)
        total = all_k.shape[0]
        outputs = []
        for sub in range(BLK // qrows):
            query_part = own_q[sub * qrows:(sub + 1) * qrows].astype(jnp.float32).reshape(qrows, HEADS, DH)
            score = jnp.einsum("qhd,khd->hqk", query_part, all_k) * scale
            qpos = sub * qrows + jnp.arange(qrows, dtype=jnp.int32)
            kpos = jnp.arange(total, dtype=jnp.int32)
            causal = kpos[None, :] <= qpos[:, None]
            outside = jnp.concatenate([jnp.zeros((BLK,), dtype=bool), extra_valid], 0)
            allowed = jnp.where(kpos[None, :] < BLK, causal, outside[None, :])
            score = jnp.where(allowed[None], score, jnp.float32(-1e30))
            top = jnp.max(score, axis=-1, keepdims=True)
            expo = jnp.where(allowed[None], jnp.exp(score - top), jnp.float32(0.0))
            weight = (expo / jnp.sum(expo, axis=-1, keepdims=True)).astype(jnp.bfloat16)
            context = jnp.einsum("hqk,khd->qhd", weight.astype(jnp.float32), all_v)
            outputs.append(context.reshape(qrows, D).astype(jnp.bfloat16))
        return jnp.concatenate(outputs, 0)

    context = lax.map(one_block, jnp.arange(blocks, dtype=jnp.int32)).reshape(FRAMES, D)
    return jnp.dot(context, w_out, preferred_element_type=jnp.float32).astype(jnp.bfloat16)
```

```python
import functools
import math

import jax
import jax.numpy as jnp
from jax import lax
from jax.experimental import pallas as pl
from jax.experimental.pallas import tpu as pltpu
from jax.sharding import PartitionSpec as P

DH = 64
PAIR = 2 * DH
WIN = 512
PK = 256
CHUNK = 1024
TILE = 256
ROWS = 512
ONES = 16
NEG = -1e30
NT = (((1,), (1,)), ((), ()))
TN = (((0,), (0,)), ((), ()))
MESH = pl.DeviceIdType.MESH


def scores(k, q):
    return lax.dot_general(k, q, NT, preferred_element_type=jnp.float32)


def attend(s, v, state):
    new = jnp.max(s, axis=0, keepdims=True)
    if state is not None:
        new = jnp.maximum(state[0], new)
    p = jnp.exp2(s - new).astype(jnp.bfloat16)
    acc = jnp.dot(v, p, preferred_element_type=jnp.float32)
    if state is not None:
        acc = acc + state[1] * jnp.exp2(state[0] - new)
    return new, acc


def kernel(
    blocks,
    sides,
    depth,
    frames_ref,
    wq_ref,
    wk_ref,
    wv_ref,
    wout_ref,
    out_ref,
    q_s,
    k_s,
    vt_s,
    wvt_s,
    pool_s,
    mine,
    far,
    ones_s,
    acc_s,
    top_s,
    ctx,
    wout_s,
    wout_sem,
    send_sem,
    recv_sem,
    xsend_sem,
    xrecv_sem,
):
    me = lax.axis_index("tm")
    side = lax.axis_index("head")
    block = frames_ref.shape[0]
    width = wq_ref.shape[1]
    pairs = width // PAIR
    chunk = min(CHUNK, block)
    chunks = block // chunk
    near = WIN // PK
    relay = blocks > 8

    load_out = pltpu.make_async_copy(
        wout_ref.at[:, pl.ds(pl.multiple_of(side * width, width), width)], wout_s, wout_sem
    )
    load_out.start()

    barrier = pltpu.get_barrier_semaphore()
    reach = [1, 2, 4] + [2**l for l in range(3, depth) if not (relay and l == 3)]
    count = sides - 1
    for d in reach:
        for there in (me + d, me - d):
            inside = jnp.logical_and(there >= 0, there < blocks)
            count = count + inside.astype(jnp.int32)

            @pl.when(inside)
            def _():
                pl.semaphore_signal(
                    barrier, inc=1, device_id={"tm": there, "head": side}, device_id_type=MESH
                )

    for s in range(1, sides):
        pl.semaphore_signal(
            barrier,
            inc=1,
            device_id={"tm": me, "head": lax.rem(side + s, sides)},
            device_id_type=MESH,
        )

    wvt_s[...] = wv_ref[...].T
    span = block // PK
    slot = lax.broadcasted_iota(jnp.int32, (PK, block), 0)
    frame = lax.broadcasted_iota(jnp.int32, (PK, block), 1)
    pool_s[...] = jnp.where(
        jnp.logical_and(frame >= slot * span, frame < slot * span + span), 1.0 / span, 0.0
    ).astype(jnp.bfloat16)
    factor = DH**-0.5 * math.log2(math.e)

    def project(i, carry):
        rows = pl.ds(pl.multiple_of(i * ROWS, ROWS), ROWS)
        f = frames_ref[rows, :]
        k = jnp.dot(f, wk_ref[...], preferred_element_type=jnp.float32).astype(jnp.bfloat16)
        q = (jnp.dot(f, wq_ref[...], preferred_element_type=jnp.float32) * factor).astype(
            jnp.bfloat16
        )
        for p in range(pairs):
            k_s[p, rows, :] = k[:, p * PAIR : (p + 1) * PAIR]
            q_s[p, rows, :] = q[:, p * PAIR : (p + 1) * PAIR]
        vt_s[:, rows] = scores(wvt_s[...], f).astype(jnp.bfloat16)
        return carry

    lax.fori_loop(0, block // ROWS, project, 0)
    pooled_v = scores(vt_s[...], pool_s[...]).astype(jnp.bfloat16)
    for p in range(pairs):
        pooled_k = jnp.dot(pool_s[...], k_s[p], preferred_element_type=jnp.float32)
        mine[p, 0, :PK, :] = pooled_k.astype(jnp.bfloat16)
        for half in range(2):
            mine[p, 0, PK + half * PAIR : PK + (half + 1) * PAIR, :] = pooled_v[
                p * PAIR : (p + 1) * PAIR, half * PAIR : (half + 1) * PAIR
            ]
        for j in range(near):
            at = block - WIN + j * PK
            mine[p, 1 + j, :PK, :] = k_s[p, at : at + PK, :]
            for half in range(2):
                first = at + half * PAIR
                mine[p, 1 + j, PK + half * PAIR : PK + (half + 1) * PAIR, :] = vt_s[
                    p * PAIR : (p + 1) * PAIR, first : first + PAIR
                ]

    for l in range(depth):
        slots = range(1 + near) if l == 0 else [near + l]
        valid = jnp.where(me >= 2**l, 1.0, 0.0).astype(jnp.bfloat16)
        for b in slots:
            ones_s[:, b * PK : (b + 1) * PK] = jnp.broadcast_to(valid, (ONES, PK))

        @pl.when(me < 2**l)
        def _():
            for p in range(pairs):
                for b in slots:
                    far[p, b, :PK, :] = jnp.broadcast_to(k_s[p, 0:1, :], (PK, PAIR))
                    far[p, b, PK:, :] = jnp.zeros((PK, PAIR), jnp.bfloat16)

    pl.semaphore_wait(barrier, count)

    def far_copy(p, kind, level, there, relayed):
        if level == 0:
            src, dst = mine.at[p], far.at[p, pl.ds(0, 1 + near)]
        elif relayed:
            src, dst = far.at[p, near + 2], far.at[p, near + level]
        else:
            src, dst = mine.at[p, 0], far.at[p, near + level]
        return pltpu.make_async_remote_copy(
            src_ref=src,
            dst_ref=dst,
            send_sem=send_sem.at[p, kind],
            recv_sem=recv_sem.at[p, level],
            device_id={"tm": there, "head": side},
            device_id_type=MESH,
        )

    direct = [(0, 0, me + 1, me + 1 < blocks), (1, 2, me + 4, me + 4 < blocks)]
    later = []
    if relay:
        low = lax.rem(me, 4) < 2
        alone = me + 4 >= blocks
        direct.append((2, 1, me + 2, jnp.logical_and(me + 2 < blocks, jnp.logical_or(low, alone))))
        later.append((3, 3, me + 4, jnp.logical_and(me >= 4, me + 4 < blocks)))
        later.append((4, 1, me - 2, jnp.logical_and(me >= 4, jnp.logical_not(low))))
    else:
        direct.append((2, 1, me + 2, me + 2 < blocks))
    for l in range(3, depth):
        if not (relay and l == 3):
            direct.append((2 + l, l, me + 2**l, me + 2**l < blocks))

    def send_far(p, carry):
        for kind, level, there, when in direct:

            @pl.when(when)
            def _():
                far_copy(p, kind, level, there, False).start()

        return carry

    lax.fori_loop(0, pairs, send_far, 0)

    def arrived(p, level):
        @pl.when(me >= 2**level)
        def _():
            far_copy(p, 0, level, me, False).wait_recv()

    first = lax.broadcasted_iota(jnp.int32, (1, PAIR), 1) < DH

    def query(p, h, c):
        q = q_s[p, c * chunk : (c + 1) * chunk, :]
        keep = jnp.broadcast_to(first == (h == 0), q.shape)
        return jnp.where(keep, q, jnp.zeros_like(q))

    causal = lax.broadcasted_iota(jnp.int32, (TILE, TILE), 0) <= lax.broadcasted_iota(
        jnp.int32, (TILE, TILE), 1
    )
    one = jnp.ones((ONES, TILE), jnp.bfloat16)

    def local(p, h):
        rows = pl.ds(pl.multiple_of(p * PAIR + h * DH, DH), DH)
        tiles = chunk // TILE
        work = [
            (c, t) for c in range(chunks) for t in range((c + 1) * tiles)
        ]
        qs = [query(p, h, c) for c in range(chunks)]

        def start(c, t):
            off = max(0, t - c * tiles) * TILE
            return scores(k_s[p, t * TILE : (t + 1) * TILE, :], qs[c][off:])

        ahead = start(*work[0])
        state = None
        for n, (c, t) in enumerate(work):
            s = ahead
            if n + 1 < len(work):
                ahead = start(*work[n + 1])
            if t == 0:
                state = None
            v = jnp.concatenate([vt_s[rows, t * TILE : (t + 1) * TILE], one], 0)
            off = max(0, t - c * tiles) * TILE
            if t >= c * tiles:
                corner = jnp.where(causal, s[:, :TILE], NEG)
                s = corner if s.shape[1] == TILE else jnp.concatenate([corner, s[:, TILE:]], 1)
            if off:
                old = [x[:, :off] for x in state]
                new = attend(s, v, tuple(x[:, off:] for x in state))
                state = tuple(jnp.concatenate(x, 1) for x in zip(old, new))
            else:
                state = attend(s, v, state)
            if t == (c + 1) * tiles - 1:
                top_s[h, c] = jnp.broadcast_to(state[0], (8, chunk))
                acc_s[h, c] = state[1]

    total = near + depth

    def distant(p, h, c):
        q = q_s[p, pl.ds(pl.multiple_of(c * chunk, chunk), chunk), :]
        keep = jnp.broadcast_to(first == (h == 0), q.shape)
        q = jnp.where(keep, q, jnp.zeros_like(q))
        state = (top_s[h, c, 0:1, :], acc_s[h, c])
        ahead = scores(far[p, 0, :PK, :], q)
        for b in range(total):
            s = ahead
            if b + 1 < total:
                ahead = scores(far[p, b + 1, :PK, :], q)
            v = jnp.concatenate(
                [
                    far[p, b, pl.ds(pl.multiple_of(PK + half * PAIR + h * DH, DH), DH), :]
                    for half in range(2)
                ],
                1,
            )
            v = jnp.concatenate([v, ones_s[:, b * PK : (b + 1) * PK]], 0)
            state = attend(s, v, state)
        acc = state[1]
        rows = pl.ds(pl.multiple_of(h * DH, DH), DH)
        ctx[side, p, c, rows, :] = (acc[:DH] / acc[DH : DH + 1]).astype(jnp.bfloat16)

    def cross(p, c, s):
        return pltpu.make_async_remote_copy(
            src_ref=ctx.at[side, p, c],
            dst_ref=ctx.at[side, p, c],
            send_sem=xsend_sem.at[p, c, s - 1],
            recv_sem=xrecv_sem.at[p, c, s - 1],
            device_id={"tm": me, "head": lax.rem(side + s, sides)},
            device_id_type=MESH,
        )

    def crossed(p, c, s):
        there = lax.rem(side + sides - s, sides)
        return pltpu.make_async_remote_copy(
            src_ref=ctx.at[there, p, c],
            dst_ref=ctx.at[there, p, c],
            send_sem=xsend_sem.at[p, c, s - 1],
            recv_sem=xrecv_sem.at[p, c, s - 1],
            device_id={"tm": me, "head": there},
            device_id_type=MESH,
        )

    def pair(p, carry):
        local(p, 0)
        arrived(p, 2)
        for kind, level, there, when in later:

            @pl.when(when)
            def _():
                far_copy(p, kind, level, there, True).start()

        local(p, 1)
        for l in range(depth):
            if l != 2:
                arrived(p, l)

        def part(c, carry):
            def head(h, carry):
                distant(p, h, c)
                return carry

            lax.fori_loop(0, 2, head, 0)
            for s in range(1, sides):
                cross(p, c, s).start()
            return carry

        lax.fori_loop(0, chunks, part, 0)
        return carry

    lax.fori_loop(0, pairs, pair, 0)
    load_out.wait()

    def finish(c, carry):
        for s in range(1, sides):

            def here(p, carry):
                crossed(p, c, s).wait_recv()
                return carry

            lax.fori_loop(0, pairs, here, 0)
        total = None
        for s in range(sides):
            for p in range(pairs):
                at = s * width + p * PAIR
                term = lax.dot_general(
                    ctx[s, p, c],
                    wout_s[at : at + PAIR, :],
                    TN,
                    preferred_element_type=jnp.float32,
                )
                total = term if total is None else total + term
        out_ref[pl.ds(pl.multiple_of(c * chunk, chunk), chunk), :] = total.astype(jnp.bfloat16)
        return carry

    lax.fori_loop(0, chunks, finish, 0)

    def settle(p, carry):
        for kind, level, there, when in direct + later:

            @pl.when(when)
            def _():
                far_copy(p, kind, level, there, (kind, level, there, when) in later).wait_send()

        def part(c, carry):
            for s in range(1, sides):
                cross(p, c, s).wait_send()
            return carry

        lax.fori_loop(0, chunks, part, 0)
        return carry

    lax.fori_loop(0, pairs, settle, 0)


def body(frames, w_query, w_key, w_value, w_out):
    block, model = frames.shape
    width = w_query.shape[1]
    pairs = width // PAIR
    blocks = lax.axis_size("tm")
    sides = lax.axis_size("head")
    depth = 0
    while 2**depth < blocks:
        depth = depth + 1
    near = WIN // PK
    chunk = min(CHUNK, block)
    chunks = block // chunk
    bf16, f32 = jnp.bfloat16, jnp.float32
    vmem = pl.BlockSpec(memory_space=pltpu.VMEM)
    pairs_total = block * block // 2 + block * PK * (near + depth)
    return pl.pallas_call(
        functools.partial(kernel, blocks, sides, depth),
        out_shape=jax.ShapeDtypeStruct((block, width), bf16),
        in_specs=[vmem] * 4 + [pl.BlockSpec(memory_space=pl.ANY)],
        out_specs=vmem,
        scratch_shapes=[
            pltpu.VMEM((pairs, block, PAIR), bf16),
            pltpu.VMEM((pairs, block, PAIR), bf16),
            pltpu.VMEM((width, block), bf16),
            pltpu.VMEM((width, model), bf16),
            pltpu.VMEM((PK, block), bf16),
            pltpu.VMEM((pairs, 1 + near, 2 * PK, PAIR), bf16),
            pltpu.VMEM((pairs, near + depth, 2 * PK, PAIR), bf16),
            pltpu.VMEM((ONES, (near + depth) * PK), bf16),
            pltpu.VMEM((2, chunks, DH + ONES, chunk), f32),
            pltpu.VMEM((2, chunks, 8, chunk), f32),
            pltpu.VMEM((sides, pairs, chunks, PAIR, chunk), bf16),
            pltpu.VMEM((model, width), bf16),
            pltpu.SemaphoreType.DMA,
            pltpu.SemaphoreType.DMA((pairs, 3 + depth)),
            pltpu.SemaphoreType.DMA((pairs, depth)),
            pltpu.SemaphoreType.DMA((pairs, chunks, max(1, sides - 1))),
            pltpu.SemaphoreType.DMA((pairs, chunks, max(1, sides - 1))),
        ],
        compiler_params=pltpu.CompilerParams(
            collective_id=0, has_side_effects=True, vmem_limit_bytes=58 * 2**20
        ),
        cost_estimate=pl.CostEstimate(
            flops=8 * width * model * block + 4 * width * pairs_total,
            bytes_accessed=4 * block * model,
            transcendentals=0,
        ),
    )(frames, w_query, w_key, w_value, w_out)


def solution(mesh):
    in_specs = (P("tm", None), P(None, "head"), P(None, "head"), P(None, "head"), P())
    out_specs = P("tm", "head")
    return jax.shard_map(body, mesh=mesh, in_specs=in_specs, out_specs=out_specs, check_vma=False)
```

```python
import functools
import math

import jax
import jax.numpy as jnp
from jax import lax
from jax.experimental import pallas as pl
from jax.experimental.pallas import tpu as pltpu
from jax.sharding import PartitionSpec as P

DH = 64
PAIR = 2 * DH
WIN = 512
PK = 256
CHUNK = 1024
TILE = 256
ROWS = 512
ONES = 16
NEG = -1e30
NT = (((1,), (1,)), ((), ()))
TN = (((0,), (0,)), ((), ()))
MESH = pl.DeviceIdType.MESH


def scores(k, q):
    return lax.dot_general(k, q, NT, preferred_element_type=jnp.float32)


def attend(s, v, state):
    new = jnp.max(s, axis=0, keepdims=True)
    if state is not None:
        new = jnp.maximum(state[0], new)
    p = jnp.exp2(s - new).astype(jnp.bfloat16)
    acc = jnp.dot(v, p, preferred_element_type=jnp.float32)
    if state is not None:
        acc = acc + state[1] * jnp.exp2(state[0] - new)
    return new, acc


def kernel(
    blocks,
    sides,
    depth,
    frames_ref,
    wq_ref,
    wk_ref,
    wv_ref,
    wout_ref,
    out_ref,
    q_s,
    k_s,
    vt_s,
    wvt_s,
    pool_s,
    mine,
    far,
    ones_s,
    acc_s,
    top_s,
    ctx,
    wout_s,
    wout_sem,
    send_sem,
    recv_sem,
    xsend_sem,
    xrecv_sem,
):
    me = lax.axis_index("tm")
    side = lax.axis_index("head")
    block = frames_ref.shape[0]
    width = wq_ref.shape[1]
    pairs = width // PAIR
    chunk = min(CHUNK, block)
    chunks = block // chunk
    near = WIN // PK
    relay = blocks > 8

    load_out = pltpu.make_async_copy(
        wout_ref.at[:, pl.ds(pl.multiple_of(side * width, width), width)], wout_s, wout_sem
    )
    load_out.start()

    barrier = pltpu.get_barrier_semaphore()
    reach = [1, 2, 4] + [2**l for l in range(3, depth) if not (relay and l == 3)]
    count = sides - 1
    for d in reach:
        for there in (me + d, me - d):
            inside = jnp.logical_and(there >= 0, there < blocks)
            count = count + inside.astype(jnp.int32)

            @pl.when(inside)
            def _():
                pl.semaphore_signal(
                    barrier, inc=1, device_id={"tm": there, "head": side}, device_id_type=MESH
                )

    for s in range(1, sides):
        pl.semaphore_signal(
            barrier,
            inc=1,
            device_id={"tm": me, "head": lax.rem(side + s, sides)},
            device_id_type=MESH,
        )

    wvt_s[...] = wv_ref[...].T
    span = block // PK
    slot = lax.broadcasted_iota(jnp.int32, (PK, block), 0)
    frame = lax.broadcasted_iota(jnp.int32, (PK, block), 1)
    pool_s[...] = jnp.where(
        jnp.logical_and(frame >= slot * span, frame < slot * span + span), 1.0 / span, 0.0
    ).astype(jnp.bfloat16)
    factor = DH**-0.5 * math.log2(math.e)

    def project(i, carry):
        rows = pl.ds(pl.multiple_of(i * ROWS, ROWS), ROWS)
        f = frames_ref[rows, :]
        k = jnp.dot(f, wk_ref[...], preferred_element_type=jnp.float32).astype(jnp.bfloat16)
        q = (jnp.dot(f, wq_ref[...], preferred_element_type=jnp.float32) * factor).astype(
            jnp.bfloat16
        )
        for p in range(pairs):
            k_s[p, rows, :] = k[:, p * PAIR : (p + 1) * PAIR]
            q_s[p, rows, :] = q[:, p * PAIR : (p + 1) * PAIR]
        vt_s[:, rows] = scores(wvt_s[...], f).astype(jnp.bfloat16)
        return carry

    lax.fori_loop(0, block // ROWS, project, 0)
    pooled_v = scores(vt_s[...], pool_s[...]).astype(jnp.bfloat16)
    for p in range(pairs):
        pooled_k = jnp.dot(pool_s[...], k_s[p], preferred_element_type=jnp.float32)
        mine[p, 0, :PK, :] = pooled_k.astype(jnp.bfloat16)
        for half in range(2):
            mine[p, 0, PK + half * PAIR : PK + (half + 1) * PAIR, :] = pooled_v[
                p * PAIR : (p + 1) * PAIR, half * PAIR : (half + 1) * PAIR
            ]
        for j in range(near):
            at = block - WIN + j * PK
            mine[p, 1 + j, :PK, :] = k_s[p, at : at + PK, :]
            for half in range(2):
                first = at + half * PAIR
                mine[p, 1 + j, PK + half * PAIR : PK + (half + 1) * PAIR, :] = vt_s[
                    p * PAIR : (p + 1) * PAIR, first : first + PAIR
                ]

    for l in range(depth):
        slots = range(1 + near) if l == 0 else [near + l]
        valid = jnp.where(me >= 2**l, 1.0, 0.0).astype(jnp.bfloat16)
        for b in slots:
            ones_s[:, b * PK : (b + 1) * PK] = jnp.broadcast_to(valid, (ONES, PK))

        @pl.when(me < 2**l)
        def _():
            for p in range(pairs):
                for b in slots:
                    far[p, b, :PK, :] = jnp.broadcast_to(k_s[p, 0:1, :], (PK, PAIR))
                    far[p, b, PK:, :] = jnp.zeros((PK, PAIR), jnp.bfloat16)

    pl.semaphore_wait(barrier, count)

    def far_copy(p, kind, level, there, relayed):
        if level == 0:
            src, dst = mine.at[p], far.at[p, pl.ds(0, 1 + near)]
        elif relayed:
            src, dst = far.at[p, near + 2], far.at[p, near + level]
        else:
            src, dst = mine.at[p, 0], far.at[p, near + level]
        return pltpu.make_async_remote_copy(
            src_ref=src,
            dst_ref=dst,
            send_sem=send_sem.at[p, kind],
            recv_sem=recv_sem.at[p, level],
            device_id={"tm": there, "head": side},
            device_id_type=MESH,
        )

    direct = [(0, 0, me + 1, me + 1 < blocks), (1, 2, me + 4, me + 4 < blocks)]
    later = []
    if relay:
        low = lax.rem(me, 4) < 2
        alone = me + 4 >= blocks
        direct.append((2, 1, me + 2, jnp.logical_and(me + 2 < blocks, jnp.logical_or(low, alone))))
        later.append((3, 3, me + 4, jnp.logical_and(me >= 4, me + 4 < blocks)))
        later.append((4, 1, me - 2, jnp.logical_and(me >= 4, jnp.logical_not(low))))
    else:
        direct.append((2, 1, me + 2, me + 2 < blocks))
    for l in range(3, depth):
        if not (relay and l == 3):
            direct.append((2 + l, l, me + 2**l, me + 2**l < blocks))

    def send_far(p):
        for kind, level, there, when in direct:

            @pl.when(when)
            def _():
                far_copy(p, kind, level, there, False).start()

    send_far(0)

    def arrived(p, level):
        @pl.when(me >= 2**level)
        def _():
            far_copy(p, 0, level, me, False).wait_recv()

    first = lax.broadcasted_iota(jnp.int32, (1, PAIR), 1) < DH

    def query(p, h, c):
        q = q_s[p, pl.ds(c * chunk if isinstance(c, int) else pl.multiple_of(c * chunk, chunk), chunk), :]
        keep = jnp.broadcast_to(first == (h == 0), q.shape)
        return jnp.where(keep, q, jnp.zeros_like(q))

    causal = lax.broadcasted_iota(jnp.int32, (TILE, TILE), 0) <= lax.broadcasted_iota(
        jnp.int32, (TILE, TILE), 1
    )
    one = jnp.ones((ONES, TILE), jnp.bfloat16)

    def local(p, h):
        rows = pl.ds(pl.multiple_of(p * PAIR + h * DH, DH), DH)
        tiles = chunk // TILE
        work = [
            (c, t) for c in range(chunks) for t in range((c + 1) * tiles)
        ]
        qs = [query(p, h, c) for c in range(chunks)]

        def start(c, t):
            off = max(0, t - c * tiles) * TILE
            return scores(k_s[p, t * TILE : (t + 1) * TILE, :], qs[c][off:])

        ahead = start(*work[0])
        state = None
        for n, (c, t) in enumerate(work):
            s = ahead
            if n + 1 < len(work):
                ahead = start(*work[n + 1])
            if t == 0:
                state = None
            v = jnp.concatenate([vt_s[rows, t * TILE : (t + 1) * TILE], one], 0)
            off = max(0, t - c * tiles) * TILE
            if t >= c * tiles:
                corner = jnp.where(causal, s[:, :TILE], NEG)
                s = corner if s.shape[1] == TILE else jnp.concatenate([corner, s[:, TILE:]], 1)
            if off:
                old = [x[:, :off] for x in state]
                new = attend(s, v, tuple(x[:, off:] for x in state))
                state = tuple(jnp.concatenate(x, 1) for x in zip(old, new))
            else:
                state = attend(s, v, state)
            if t == (c + 1) * tiles - 1:
                top_s[2 * lax.rem(p, 2) + h, c] = jnp.broadcast_to(state[0], (8, chunk))
                acc_s[2 * lax.rem(p, 2) + h, c] = state[1]

    total = near + depth

    def distant(p, h, c):
        q = query(p, h, c)
        held = 2 * lax.rem(p, 2) + h
        state = (top_s[held, c, 0:1, :], acc_s[held, c])
        ahead = scores(far[p, 0, :PK, :], q)
        for b in range(total):
            s = ahead
            if b + 1 < total:
                ahead = scores(far[p, b + 1, :PK, :], q)
            v = jnp.concatenate(
                [
                    far[p, b, pl.ds(pl.multiple_of(PK + half * PAIR + h * DH, DH), DH), :]
                    for half in range(2)
                ],
                1,
            )
            v = jnp.concatenate([v, ones_s[:, b * PK : (b + 1) * PK]], 0)
            state = attend(s, v, state)
        acc = state[1]
        rows = pl.ds(pl.multiple_of(h * DH, DH), DH)
        ctx[side, p, c, rows, :] = (acc[:DH] / acc[DH : DH + 1]).astype(jnp.bfloat16)

    def cross(p, c, s):
        return pltpu.make_async_remote_copy(
            src_ref=ctx.at[side, p, c],
            dst_ref=ctx.at[side, p, c],
            send_sem=xsend_sem.at[p, c, s - 1],
            recv_sem=xrecv_sem.at[p, c, s - 1],
            device_id={"tm": me, "head": lax.rem(side + s, sides)},
            device_id_type=MESH,
        )

    def crossed(p, c, s):
        there = lax.rem(side + sides - s, sides)
        return pltpu.make_async_remote_copy(
            src_ref=ctx.at[there, p, c],
            dst_ref=ctx.at[there, p, c],
            send_sem=xsend_sem.at[p, c, s - 1],
            recv_sem=xrecv_sem.at[p, c, s - 1],
            device_id={"tm": me, "head": there},
            device_id_type=MESH,
        )

    def step(n, carry):
        @pl.when(n < pairs)
        def _():
            def head(h, carry):
                local(n, h)
                return carry

            lax.fori_loop(0, 2, head, 0)
            arrived(n, 2)
            for kind, level, there, when in later:

                @pl.when(when)
                def _():
                    far_copy(n, kind, level, there, True).start()

            @pl.when(n + 1 < pairs)
            def _():
                send_far(n + 1)

        @pl.when(n >= 1)
        def _():
            p = n - 1
            for l in range(depth):
                if l != 2:
                    arrived(p, l)

            def part(c, carry):
                def head(h, carry):
                    distant(p, h, c)
                    return carry

                lax.fori_loop(0, 2, head, 0)
                for s in range(1, sides):
                    cross(p, c, s).start()
                return carry

            lax.fori_loop(0, chunks, part, 0)

        return carry

    lax.fori_loop(0, pairs + 1, step, 0)
    load_out.wait()

    def finish(c, carry):
        for s in range(1, sides):

            def here(p, carry):
                crossed(p, c, s).wait_recv()
                return carry

            lax.fori_loop(0, pairs, here, 0)
        total = None
        for s in range(sides):
            for p in range(pairs):
                at = s * width + p * PAIR
                term = lax.dot_general(
                    ctx[s, p, c],
                    wout_s[at : at + PAIR, :],
                    TN,
                    preferred_element_type=jnp.float32,
                )
                total = term if total is None else total + term
        out_ref[pl.ds(pl.multiple_of(c * chunk, chunk), chunk), :] = total.astype(jnp.bfloat16)
        return carry

    lax.fori_loop(0, chunks, finish, 0)

    def settle(p, carry):
        for kind, level, there, when in direct + later:

            @pl.when(when)
            def _():
                far_copy(p, kind, level, there, (kind, level, there, when) in later).wait_send()

        def part(c, carry):
            for s in range(1, sides):
                cross(p, c, s).wait_send()
            return carry

        lax.fori_loop(0, chunks, part, 0)
        return carry

    lax.fori_loop(0, pairs, settle, 0)


def body(frames, w_query, w_key, w_value, w_out):
    block, model = frames.shape
    width = w_query.shape[1]
    pairs = width // PAIR
    blocks = lax.axis_size("tm")
    sides = lax.axis_size("head")
    depth = 0
    while 2**depth < blocks:
        depth = depth + 1
    near = WIN // PK
    chunk = min(CHUNK, block)
    chunks = block // chunk
    bf16, f32 = jnp.bfloat16, jnp.float32
    vmem = pl.BlockSpec(memory_space=pltpu.VMEM)
    pairs_total = block * block // 2 + block * PK * (near + depth)
    return pl.pallas_call(
        functools.partial(kernel, blocks, sides, depth),
        out_shape=jax.ShapeDtypeStruct((block, width), bf16),
        in_specs=[vmem] * 4 + [pl.BlockSpec(memory_space=pl.ANY)],
        out_specs=vmem,
        scratch_shapes=[
            pltpu.VMEM((pairs, block, PAIR), bf16),
            pltpu.VMEM((pairs, block, PAIR), bf16),
            pltpu.VMEM((width, block), bf16),
            pltpu.VMEM((width, model), bf16),
            pltpu.VMEM((PK, block), bf16),
            pltpu.VMEM((pairs, 1 + near, 2 * PK, PAIR), bf16),
            pltpu.VMEM((pairs, near + depth, 2 * PK, PAIR), bf16),
            pltpu.VMEM((ONES, (near + depth) * PK), bf16),
            pltpu.VMEM((4, chunks, DH + ONES, chunk), f32),
            pltpu.VMEM((4, chunks, 8, chunk), f32),
            pltpu.VMEM((sides, pairs, chunks, PAIR, chunk), bf16),
            pltpu.VMEM((model, width), bf16),
            pltpu.SemaphoreType.DMA,
            pltpu.SemaphoreType.DMA((pairs, 3 + depth)),
            pltpu.SemaphoreType.DMA((pairs, depth)),
            pltpu.SemaphoreType.DMA((pairs, chunks, max(1, sides - 1))),
            pltpu.SemaphoreType.DMA((pairs, chunks, max(1, sides - 1))),
        ],
        compiler_params=pltpu.CompilerParams(
            collective_id=0, has_side_effects=True, vmem_limit_bytes=58 * 2**20
        ),
        cost_estimate=pl.CostEstimate(
            flops=8 * width * model * block + 4 * width * pairs_total,
            bytes_accessed=4 * block * model,
            transcendentals=0,
        ),
    )(frames, w_query, w_key, w_value, w_out)


def solution(mesh):
    in_specs = (P("tm", None), P(None, "head"), P(None, "head"), P(None, "head"), P())
    out_specs = P("tm", "head")
    return jax.shard_map(body, mesh=mesh, in_specs=in_specs, out_specs=out_specs, check_vma=False)
```

```python
import functools
import math

import jax
import jax.numpy as jnp
from jax import lax
from jax.experimental import pallas as pl
from jax.experimental.pallas import tpu as pltpu
from jax.sharding import PartitionSpec as P

DH = 64
PAIR = 2 * DH
WIN = 512
PK = 256
CHUNK = 1024
DIAG = 512
SPAN = 2048
ROWS = 512
ONES = 16
NEG = -1e30
ABOVE = 90.0
ROOM = 100.0
LARGE = 2000.0
GROUP = 3
NT = (((1,), (1,)), ((), ()))
TN = (((0,), (0,)), ((), ()))
MESH = pl.DeviceIdType.MESH


def scores(k, q):
    return lax.dot_general(k, q, NT, preferred_element_type=jnp.float32)


def attend(s, v, state):
    new = jnp.max(s, axis=0, keepdims=True)
    if state is not None:
        new = jnp.maximum(state[0], new)
    p = jnp.exp2(s - new).astype(jnp.bfloat16)
    acc = jnp.dot(v, p, preferred_element_type=jnp.float32)
    if state is not None:
        acc = acc + state[1] * jnp.exp2(state[0] - new)
    return new, acc


def kernel(
    exact,
    blocks,
    sides,
    depth,
    frames_in,
    wq_in,
    wk_in,
    wv_in,
    wout_ref,
    out_ref,
    flag_ref,
    frames_ref,
    wq_ref,
    wk_ref,
    wv_ref,
    q_s,
    k_s,
    vt_s,
    wvt_s,
    pooled_s,
    shift_s,
    norm_s,
    kmax_s,
    flag_s,
    flag_r,
    flag_x,
    mine,
    far,
    ones_s,
    acc_s,
    top_s,
    ctx,
    wout_s,
    wout_sem,
    in_sem,
    fsend_sem,
    frecv_sem,
    send_sem,
    recv_sem,
    xsend_sem,
    xrecv_sem,
):
    me = lax.axis_index("tm")
    side = lax.axis_index("head")
    block = frames_ref.shape[0]
    width = wq_ref.shape[1]
    pairs = width // PAIR
    chunk = min(CHUNK, block)
    chunks = block // chunk
    near = WIN // PK
    relay = blocks > 8

    load_out = pltpu.make_async_copy(
        wout_ref.at[:, pl.ds(pl.multiple_of(side * width, width), width)], wout_s, wout_sem
    )

    steps = block // ROWS

    def load(i):
        if i < 3:
            refs = [(wk_in, wk_ref), (wq_in, wq_ref), (wv_in, wv_ref)]
            return pltpu.make_async_copy(*refs[i], in_sem.at[i])

    def load_rows(i):
        rows = pl.ds(pl.multiple_of(i * ROWS, ROWS), ROWS)
        return pltpu.make_async_copy(frames_in.at[rows], frames_ref.at[rows], in_sem.at[3 + i])

    load(2).start()
    load(0).start()
    load_rows(steps - 1).start()
    load(1).start()
    for i in range(steps - 1):
        load_rows(i).start()
    load_out.start()

    barrier = pltpu.get_barrier_semaphore()
    reach = [2**l for l in range(depth)]
    count = sides - 1
    for d in reach:
        for there in (me + d, me - d):
            inside = jnp.logical_and(there >= 0, there < blocks)
            count = count + inside.astype(jnp.int32)

            @pl.when(inside)
            def _():
                pl.semaphore_signal(
                    barrier, inc=1, device_id={"tm": there, "head": side}, device_id_type=MESH
                )

    for s in range(1, sides):
        pl.semaphore_signal(
            barrier,
            inc=1,
            device_id={"tm": me, "head": lax.rem(side + s, sides)},
            device_id_type=MESH,
        )

    span = block // PK
    slots_in = ROWS // span
    slot = lax.broadcasted_iota(jnp.int32, (slots_in, ROWS), 0) * span
    frame = lax.broadcasted_iota(jnp.int32, (slots_in, ROWS), 1)
    pool = jnp.where(
        jnp.logical_and(frame >= slot, frame < slot + span), 1.0 / span, 0.0
    ).astype(jnp.bfloat16)
    column = lax.broadcasted_iota(jnp.int32, (width, PAIR), 0)
    owner = lax.broadcasted_iota(jnp.int32, (width, PAIR), 1) * DH
    by_head = jnp.where(
        jnp.logical_and(column >= owner, column < owner + DH), 1.0, 0.0
    ).astype(jnp.bfloat16)
    factor = DH**-0.5 * math.log2(math.e)
    kmax_s[...] = jnp.zeros_like(kmax_s)
    load(2).wait()
    wvt_s[...] = wv_ref[...].T
    load(0).wait()
    load_rows(steps - 1).wait()
    load(1).wait()

    def heads(x):
        return jnp.dot(x.astype(jnp.bfloat16), by_head, preferred_element_type=jnp.float32)

    def project(i, carry):
        rows = pl.ds(pl.multiple_of(i * ROWS, ROWS), ROWS)
        f = frames_ref[rows, :]
        kf = jnp.dot(f, wk_ref[...], preferred_element_type=jnp.float32)
        qf = jnp.dot(f, wq_ref[...], preferred_element_type=jnp.float32) * factor
        k, q = kf.astype(jnp.bfloat16), qf.astype(jnp.bfloat16)
        for p in range(pairs):
            k_s[p, rows, :] = k[:, p * PAIR : (p + 1) * PAIR]
            q_s[p, rows, :] = q[:, p * PAIR : (p + 1) * PAIR]
        if not exact:
            longest = jnp.max(heads(kf * kf), axis=0, keepdims=True)
            kmax_s[...] = jnp.maximum(kmax_s[...], jnp.broadcast_to(longest, kmax_s.shape))
            norm_s[rows, :] = heads(qf * qf)
            shift_s[rows, :] = (-ABOVE - heads(qf * kf)).astype(jnp.bfloat16)
        v = scores(wvt_s[...], f).astype(jnp.bfloat16)
        vt_s[:, rows] = v
        return carry

    project(steps - 1, 0)
    for i in range(steps):
        if i < steps - 1:
            load_rows(i).wait()
        pooled_s[i * slots_in : (i + 1) * slots_in, :] = jnp.dot(
            pool, frames_ref[i * ROWS : (i + 1) * ROWS, :], preferred_element_type=jnp.float32
        ).astype(jnp.bfloat16)
    pooled_k = jnp.dot(pooled_s[...], wk_ref[...], preferred_element_type=jnp.float32)
    pooled_k = pooled_k.astype(jnp.bfloat16)
    pooled_v = scores(wvt_s[...], pooled_s[...]).astype(jnp.bfloat16)
    for p in range(pairs):
        mine[p, 0, :PK, :] = pooled_k[:, p * PAIR : (p + 1) * PAIR]
        for half in range(2):
            mine[p, 0, PK + half * PAIR : PK + (half + 1) * PAIR, :] = pooled_v[
                p * PAIR : (p + 1) * PAIR, half * PAIR : (half + 1) * PAIR
            ]
        for j in range(near):
            at = block - WIN + j * PK
            mine[p, 1 + j, :PK, :] = k_s[p, at : at + PK, :]
            for half in range(2):
                first = at + half * PAIR
                mine[p, 1 + j, PK + half * PAIR : PK + (half + 1) * PAIR, :] = vt_s[
                    p * PAIR : (p + 1) * PAIR, first : first + PAIR
                ]

    pl.semaphore_wait(barrier, count)

    def far_copy(p, kind, level, there, relayed):
        if level == 0:
            src, dst = mine.at[p], far.at[p, pl.ds(0, 1 + near)]
        elif relayed:
            src, dst = far.at[p, near + 2], far.at[p, near + level]
        else:
            src, dst = mine.at[p, 0], far.at[p, near + level]
        return pltpu.make_async_remote_copy(
            src_ref=src,
            dst_ref=dst,
            send_sem=send_sem.at[p, kind],
            recv_sem=recv_sem.at[p, level],
            device_id={"tm": there, "head": side},
            device_id_type=MESH,
        )

    direct = [(0, 0, me + 1, me + 1 < blocks), (1, 2, me + 4, me + 4 < blocks)]
    later = []
    if relay:
        low = lax.rem(me, 4) < 2
        alone = me + 4 >= blocks
        direct.append((2, 1, me + 2, jnp.logical_and(me + 2 < blocks, jnp.logical_or(low, alone))))
        later.append((3, 3, me + 4, jnp.logical_and(me >= 4, me + 4 < blocks)))
        later.append((4, 1, me - 2, jnp.logical_and(me >= 4, jnp.logical_not(low))))
    else:
        direct.append((2, 1, me + 2, me + 2 < blocks))
    for l in range(3, depth):
        if not (relay and l == 3):
            direct.append((2 + l, l, me + 2**l, me + 2**l < blocks))

    def send_far(p):
        for kind, level, there, when in direct:

            @pl.when(when)
            def _():
                far_copy(p, kind, level, there, False).start()

    send_far(0)
    lax.fori_loop(0, steps - 1, project, 0)

    for l in range(depth):
        slots = range(1 + near) if l == 0 else [near + l]
        valid = jnp.where(me >= 2**l, 1.0, 0.0).astype(jnp.bfloat16)
        for b in slots:
            ones_s[:, b * PK : (b + 1) * PK] = jnp.broadcast_to(valid, (ONES, PK))

        @pl.when(me < 2**l)
        def _():
            for p in range(pairs):
                for b in slots:
                    far[p, b, :PK, :] = jnp.broadcast_to(k_s[p, 0:1, :], (PK, PAIR))
                    far[p, b, PK:, :] = jnp.zeros((PK, PAIR), jnp.bfloat16)

    def arrived(p, level):
        @pl.when(me >= 2**level)
        def _():
            far_copy(p, 0, level, me, False).wait_recv()

    def pass_on(p):
        arrived(p, 2)
        for kind, level, there, when in later:

            @pl.when(when)
            def _():
                far_copy(p, kind, level, there, True).start()

    pass_on(0)
    if pairs > 1:
        send_far(1)

    first = lax.broadcasted_iota(jnp.int32, (1, PAIR), 1) < DH

    def query(p, h, c):
        rows = pl.ds(c * chunk if isinstance(c, int) else pl.multiple_of(c * chunk, chunk), chunk)
        q = q_s[p, rows, :]
        keep = jnp.broadcast_to(first == (h == 0), q.shape)
        q = jnp.where(keep, q, jnp.zeros_like(q))
        return q if exact else jnp.concatenate([q, shift_s[rows, :]], 1)

    lane = lax.broadcasted_iota(jnp.int32, (1, PAIR), 1)

    def key(k, p, h):
        if exact:
            return k
        pick = jnp.where(lane == 2 * p + h, 1.0, 0.0).astype(jnp.bfloat16)
        return jnp.concatenate([k, jnp.broadcast_to(pick, k.shape)], 1)

    def fold(s, v, state):
        if exact:
            return attend(s, v, state)
        acc = jnp.dot(v, jnp.exp2(s).astype(jnp.bfloat16), preferred_element_type=jnp.float32)
        return (acc,) if state is None else (state[0] + acc,)

    def ones(columns):
        return jnp.ones((ONES, columns), jnp.bfloat16)

    causal = lax.broadcasted_iota(jnp.int32, (DIAG, DIAG), 0) <= lax.broadcasted_iota(
        jnp.int32, (DIAG, DIAG), 1
    )

    def local(p, h):
        vrows = pl.ds(pl.multiple_of(p * PAIR + h * DH, DH), DH)
        for c in range(chunks):
            q = query(p, h, c)
            for t in range(0, chunk, DIAG):
                state = None
                end = c * chunk + t + DIAG
                for at in range(0, end, SPAN):
                    count = min(SPAN, end - at)
                    s = scores(key(k_s[p, at : at + count, :], p, h), q[t : t + DIAG])
                    v = jnp.concatenate([vt_s[vrows, at : at + count], ones(count)], 0)
                    if at + count == end:
                        corner = jnp.where(causal, s[count - DIAG :], NEG)
                        s = jnp.concatenate([s[: count - DIAG], corner], 0) if count > DIAG else corner
                    state = fold(s, v, state)
                acc_s[h, c, :, t : t + DIAG] = state[-1]
                if exact:
                    top_s[h, c, :, t : t + DIAG] = jnp.broadcast_to(state[0], (8, DIAG))

    total = near + depth

    def distant(p, h, c):
        q = query(p, h, c)
        held = h
        state = (top_s[held, c, 0:1, :], acc_s[held, c]) if exact else (acc_s[held, c],)
        for b in range(0, total, GROUP):
            group = range(b, min(b + GROUP, total))
            k = jnp.concatenate([far[p, g, :PK, :] for g in group], 0)
            s = scores(key(k, p, h), q)
            v = jnp.concatenate(
                [
                    far[p, g, pl.ds(pl.multiple_of(PK + half * PAIR + h * DH, DH), DH), :]
                    for g in group
                    for half in range(2)
                ],
                1,
            )
            v = jnp.concatenate([v, ones_s[:, b * PK : b * PK + len(group) * PK]], 0)
            state = fold(s, v, state)
        acc = state[-1]
        rows = pl.ds(pl.multiple_of(h * DH, DH), DH)
        ctx[side, p, c, rows, :] = (acc[:DH] / acc[DH : DH + 1]).astype(jnp.bfloat16)

    def check():
        longest = jnp.sqrt(jnp.maximum(flag_s[depth - 1, 0:1], flag_r[depth - 1, 0:1])) * 1.01
        bound = jnp.sqrt(norm_s[...]) * 1.01 * longest
        over = jnp.maximum(bound + shift_s[...].astype(jnp.float32) - ROOM, bound - LARGE)
        flag_s[depth] = jnp.broadcast_to(jnp.max(over, axis=0, keepdims=True), flag_s.shape[1:])

    def tell(r):
        d = 2 ** (r % depth)
        there = me + d * (1 - 2 * lax.rem(me // d, 2))
        return pltpu.make_async_remote_copy(
            src_ref=flag_s.at[r],
            dst_ref=flag_r.at[r],
            send_sem=fsend_sem.at[r],
            recv_sem=frecv_sem.at[r],
            device_id={"tm": there, "head": side},
            device_id_type=MESH,
        )

    def heard(r):
        tell(r).wait()
        if r == depth - 1:
            check()
        else:
            flag_s[r + 1] = jnp.maximum(flag_s[r], flag_r[r])

    def spread(r):
        if r == 0:
            flag_s[0] = kmax_s[...]
        else:
            heard(r - 1)
        tell(r).start()

    def tell_side(s):
        return pltpu.make_async_remote_copy(
            src_ref=flag_s.at[2 * depth],
            dst_ref=flag_x.at[s - 1],
            send_sem=fsend_sem.at[2 * depth + s - 1],
            recv_sem=frecv_sem.at[2 * depth + s - 1],
            device_id={"tm": me, "head": lax.rem(side + s, sides)},
            device_id_type=MESH,
        )

    def cross(p, c, h, s):
        rows = pl.ds(pl.multiple_of(h * DH, DH), DH)
        return pltpu.make_async_remote_copy(
            src_ref=ctx.at[side, p, c, rows],
            dst_ref=ctx.at[side, p, c, rows],
            send_sem=xsend_sem.at[p, 2 * c + h, s - 1],
            recv_sem=xrecv_sem.at[p, 2 * c + h, s - 1],
            device_id={"tm": me, "head": lax.rem(side + s, sides)},
            device_id_type=MESH,
        )

    def crossed(p, c, h, s):
        rows = pl.ds(pl.multiple_of(h * DH, DH), DH)
        there = lax.rem(side + sides - s, sides)
        return pltpu.make_async_remote_copy(
            src_ref=ctx.at[there, p, c, rows],
            dst_ref=ctx.at[there, p, c, rows],
            send_sem=xsend_sem.at[p, 2 * c + h, s - 1],
            recv_sem=xrecv_sem.at[p, 2 * c + h, s - 1],
            device_id={"tm": me, "head": there},
            device_id_type=MESH,
        )

    turns = 2 * pairs
    rounds = 2 * depth

    def step(p, carry):
        def own(h, carry):
            if not exact:
                for r in range(min(rounds, turns)):

                    @pl.when(2 * p + h == r)
                    def _():
                        spread(r)

            local(p, h)
            return carry

        lax.fori_loop(0, 2, own, 0)

        @pl.when(p + 1 < pairs)
        def _():
            pass_on(p + 1)

        @pl.when(p + 2 < pairs)
        def _():
            send_far(p + 2)

        for l in range(depth):
            if l != 2:
                arrived(p, l)

        def part(c, carry):
            def head(h, carry):
                distant(p, h, c)
                for s in range(1, sides):
                    cross(p, c, h, s).start()
                return carry

            lax.fori_loop(0, 2, head, 0)
            return carry

        lax.fori_loop(0, chunks, part, 0)
        return carry

    lax.fori_loop(0, pairs, step, 0)
    load_out.wait()
    if not exact:
        for r in range(turns, rounds):
            spread(r)
        heard(rounds - 1)
        for x in range(1, sides):
            tell_side(x).start()

    def finish(c, carry):
        def product(x):
            weights = wout_s[pl.ds(pl.multiple_of(x * width, width), width), :]
            context = ctx[x, :, c].reshape(width, chunk)
            return lax.dot_general(context, weights, TN, preferred_element_type=jnp.float32)

        total = product(side)
        for s in range(1, sides):

            def here(n, carry):
                crossed(n // 2, c, lax.rem(n, 2), s).wait_recv()
                return carry

            lax.fori_loop(0, 2 * pairs, here, 0)
            total = total + product(lax.rem(side + sides - s, sides))
        out_ref[pl.ds(pl.multiple_of(c * chunk, chunk), chunk), :] = total.astype(jnp.bfloat16)
        return carry

    lax.fori_loop(0, chunks, finish, 0)
    if exact:
        flag_ref[...] = jnp.zeros_like(flag_ref)
    else:
        worst = flag_s[2 * depth]
        for x in range(1, sides):
            tell_side(x).wait()
            worst = jnp.maximum(worst, flag_x[x - 1])
        flag_ref[...] = jnp.broadcast_to(jnp.max(worst, axis=1, keepdims=True), flag_ref.shape)

    def settle(p, carry):
        for kind, level, there, when in direct + later:

            @pl.when(when)
            def _():
                far_copy(p, kind, level, there, (kind, level, there, when) in later).wait_send()

        def part(n, carry):
            for s in range(1, sides):
                cross(p, n // 2, lax.rem(n, 2), s).wait_send()
            return carry

        lax.fori_loop(0, 2 * chunks, part, 0)
        return carry

    lax.fori_loop(0, pairs, settle, 0)


def run(exact, frames, w_query, w_key, w_value, w_out):
    block, model = frames.shape
    width = w_query.shape[1]
    pairs = width // PAIR
    blocks = lax.axis_size("tm")
    sides = lax.axis_size("head")
    depth = 0
    while 2**depth < blocks:
        depth = depth + 1
    near = WIN // PK
    chunk = min(CHUNK, block)
    chunks = block // chunk
    others = max(1, sides - 1)
    bf16, f32 = jnp.bfloat16, jnp.float32
    anywhere = pl.BlockSpec(memory_space=pl.ANY)
    vmem = pl.BlockSpec(memory_space=pltpu.VMEM)
    scored = block * block // 2 + block * PK * (near + depth)
    blob = 2 * PK
    return pl.pallas_call(
        functools.partial(kernel, exact, blocks, sides, depth),
        out_shape=[
            jax.ShapeDtypeStruct((block, width), bf16),
            jax.ShapeDtypeStruct((8, PAIR), f32),
        ],
        in_specs=[anywhere] * 5,
        out_specs=[vmem, vmem],
        scratch_shapes=[
            pltpu.VMEM((block, model), bf16),
            pltpu.VMEM((model, width), bf16),
            pltpu.VMEM((model, width), bf16),
            pltpu.VMEM((model, width), bf16),
            pltpu.VMEM((pairs, block, PAIR), bf16),
            pltpu.VMEM((pairs, block, PAIR), bf16),
            pltpu.VMEM((width, block), bf16),
            pltpu.VMEM((width, model), bf16),
            pltpu.VMEM((PK, model), bf16),
            pltpu.VMEM((block, PAIR), bf16),
            pltpu.VMEM((block, PAIR), f32),
            pltpu.VMEM((8, PAIR), f32),
            pltpu.VMEM((2 * depth + 1, 8, PAIR), f32),
            pltpu.VMEM((2 * depth, 8, PAIR), f32),
            pltpu.VMEM((others, 8, PAIR), f32),
            pltpu.VMEM((pairs, 1 + near, blob, PAIR), bf16),
            pltpu.VMEM((pairs, near + depth, blob, PAIR), bf16),
            pltpu.VMEM((ONES, (near + depth) * PK), bf16),
            pltpu.VMEM((2, chunks, DH + ONES, chunk), f32),
            pltpu.VMEM((2, chunks, 8, chunk), f32),
            pltpu.VMEM((sides, pairs, chunks, PAIR, chunk), bf16),
            pltpu.VMEM((model, width), bf16),
            pltpu.SemaphoreType.DMA,
            pltpu.SemaphoreType.DMA((3 + block // ROWS,)),
            pltpu.SemaphoreType.DMA((2 * depth + others,)),
            pltpu.SemaphoreType.DMA((2 * depth + others,)),
            pltpu.SemaphoreType.DMA((pairs, 3 + depth)),
            pltpu.SemaphoreType.DMA((pairs, depth)),
            pltpu.SemaphoreType.DMA((pairs, 2 * chunks, others)),
            pltpu.SemaphoreType.DMA((pairs, 2 * chunks, others)),
        ],
        compiler_params=pltpu.CompilerParams(
            collective_id=int(exact), has_side_effects=True, vmem_limit_bytes=58 * 2**20
        ),
        cost_estimate=pl.CostEstimate(
            flops=8 * width * model * block + 4 * width * scored,
            bytes_accessed=4 * block * model,
            transcendentals=0,
        ),
    )(frames, w_query, w_key, w_value, w_out)


def body(*args):
    out, over = run(False, *args)
    return lax.cond(over[0, 0] > 0, lambda: run(True, *args)[0], lambda: out)


def solution(mesh):
    in_specs = (P("tm", None), P(None, "head"), P(None, "head"), P(None, "head"), P())
    out_specs = P("tm", "head")
    return jax.shard_map(body, mesh=mesh, in_specs=in_specs, out_specs=out_specs, check_vma=False)
```

```python
import functools
import math

import jax
import jax.numpy as jnp
from jax import lax
from jax.experimental import pallas as pl
from jax.experimental.pallas import tpu as pltpu
from jax.sharding import PartitionSpec as P

DH = 64
PAIR = 2 * DH
WIN = 512
PK = 256
CHUNK = 1024
DIAG = 512
SPAN = 2048
ROWS = 512
ONES = 16
NEG = -1e30
ABOVE = 90.0
ROOM = 100.0
LARGE = 2000.0
GROUP = 3
NT = (((1,), (1,)), ((), ()))
TN = (((0,), (0,)), ((), ()))
MESH = pl.DeviceIdType.MESH


def scores(k, q):
    return lax.dot_general(k, q, NT, preferred_element_type=jnp.float32)


def attend(s, v, state):
    new = jnp.max(s, axis=0, keepdims=True)
    if state is not None:
        new = jnp.maximum(state[0], new)
    p = jnp.exp2(s - new).astype(jnp.bfloat16)
    acc = jnp.dot(v, p, preferred_element_type=jnp.float32)
    if state is not None:
        acc = acc + state[1] * jnp.exp2(state[0] - new)
    return new, acc


def kernel(
    exact,
    blocks,
    sides,
    depth,
    frames_in,
    wq_in,
    wk_in,
    wv_in,
    wout_ref,
    out_ref,
    flag_ref,
    frames_ref,
    wq_ref,
    wk_ref,
    wv_ref,
    q_s,
    k_s,
    vt_s,
    wvt_s,
    pooled_s,
    shift_s,
    norm_s,
    kmax_s,
    flag_s,
    flag_r,
    flag_x,
    mine,
    far,
    ones_s,
    acc_s,
    top_s,
    ctx,
    wout_s,
    wout_sem,
    in_sem,
    fsend_sem,
    frecv_sem,
    send_sem,
    recv_sem,
    xsend_sem,
    xrecv_sem,
):
    me = lax.axis_index("tm")
    side = lax.axis_index("head")
    block = frames_ref.shape[0]
    width = wq_ref.shape[1]
    pairs = width // PAIR
    chunk = min(CHUNK, block)
    chunks = block // chunk
    near = WIN // PK
    relay = blocks > 8

    load_out = pltpu.make_async_copy(
        wout_ref.at[:, pl.ds(pl.multiple_of(side * width, width), width)], wout_s, wout_sem
    )

    steps = block // ROWS

    def load(i):
        if i < 3:
            refs = [(wk_in, wk_ref), (wq_in, wq_ref), (wv_in, wv_ref)]
            return pltpu.make_async_copy(*refs[i], in_sem.at[i])

    def load_rows(i):
        rows = pl.ds(pl.multiple_of(i * ROWS, ROWS), ROWS)
        return pltpu.make_async_copy(frames_in.at[rows], frames_ref.at[rows], in_sem.at[3 + i])

    load(2).start()
    load(0).start()
    load_rows(steps - 1).start()
    load(1).start()
    for i in range(steps - 1):
        load_rows(i).start()
    load_out.start()

    barrier = pltpu.get_barrier_semaphore()
    reach = [2**l for l in range(depth)]
    count = sides - 1
    for d in reach:
        for there in (me + d, me - d):
            inside = jnp.logical_and(there >= 0, there < blocks)
            count = count + inside.astype(jnp.int32)

            @pl.when(inside)
            def _():
                pl.semaphore_signal(
                    barrier, inc=1, device_id={"tm": there, "head": side}, device_id_type=MESH
                )

    for s in range(1, sides):
        pl.semaphore_signal(
            barrier,
            inc=1,
            device_id={"tm": me, "head": lax.rem(side + s, sides)},
            device_id_type=MESH,
        )

    span = block // PK
    slots_in = ROWS // span
    slot = lax.broadcasted_iota(jnp.int32, (slots_in, ROWS), 0) * span
    frame = lax.broadcasted_iota(jnp.int32, (slots_in, ROWS), 1)
    pool = jnp.where(
        jnp.logical_and(frame >= slot, frame < slot + span), 1.0 / span, 0.0
    ).astype(jnp.bfloat16)
    column = lax.broadcasted_iota(jnp.int32, (width, PAIR), 0)
    owner = lax.broadcasted_iota(jnp.int32, (width, PAIR), 1) * DH
    by_head = jnp.where(
        jnp.logical_and(column >= owner, column < owner + DH), 1.0, 0.0
    ).astype(jnp.bfloat16)
    factor = DH**-0.5 * math.log2(math.e)
    kmax_s[...] = jnp.zeros_like(kmax_s)
    load(2).wait()
    wvt_s[...] = wv_ref[...].T
    load(0).wait()
    load_rows(steps - 1).wait()
    load(1).wait()

    def heads(x):
        return jnp.dot(x.astype(jnp.bfloat16), by_head, preferred_element_type=jnp.float32)

    def project(i, carry):
        rows = pl.ds(pl.multiple_of(i * ROWS, ROWS), ROWS)
        f = frames_ref[rows, :]
        kf = jnp.dot(f, wk_ref[...], preferred_element_type=jnp.float32)
        qf = jnp.dot(f, wq_ref[...], preferred_element_type=jnp.float32) * factor
        k, q = kf.astype(jnp.bfloat16), qf.astype(jnp.bfloat16)
        for p in range(pairs):
            k_s[p, rows, :] = k[:, p * PAIR : (p + 1) * PAIR]
            q_s[p, rows, :] = q[:, p * PAIR : (p + 1) * PAIR]
        if not exact:
            longest = jnp.max(heads(kf * kf), axis=0, keepdims=True)
            kmax_s[...] = jnp.maximum(kmax_s[...], jnp.broadcast_to(longest, kmax_s.shape))
            norm_s[rows, :] = heads(qf * qf)
            shift_s[rows, :] = (-ABOVE - heads(qf * kf)).astype(jnp.bfloat16)
        v = scores(wvt_s[...], f).astype(jnp.bfloat16)
        vt_s[:, rows] = v
        return carry

    project(steps - 1, 0)
    for i in range(steps):
        if i < steps - 1:
            load_rows(i).wait()
        pooled_s[i * slots_in : (i + 1) * slots_in, :] = jnp.dot(
            pool, frames_ref[i * ROWS : (i + 1) * ROWS, :], preferred_element_type=jnp.float32
        ).astype(jnp.bfloat16)
    pooled_k = jnp.dot(pooled_s[...], wk_ref[...], preferred_element_type=jnp.float32)
    pooled_k = pooled_k.astype(jnp.bfloat16)
    pooled_v = scores(wvt_s[...], pooled_s[...]).astype(jnp.bfloat16)
    for p in range(pairs):
        mine[p, 0, :PK, :] = pooled_k[:, p * PAIR : (p + 1) * PAIR]
        for half in range(2):
            mine[p, 0, PK + half * PAIR : PK + (half + 1) * PAIR, :] = pooled_v[
                p * PAIR : (p + 1) * PAIR, half * PAIR : (half + 1) * PAIR
            ]
        for j in range(near):
            at = block - WIN + j * PK
            mine[p, 1 + j, :PK, :] = k_s[p, at : at + PK, :]
            for half in range(2):
                first = at + half * PAIR
                mine[p, 1 + j, PK + half * PAIR : PK + (half + 1) * PAIR, :] = vt_s[
                    p * PAIR : (p + 1) * PAIR, first : first + PAIR
                ]

    pl.semaphore_wait(barrier, count)

    def far_copy(p, kind, level, there, relayed):
        if level == 0:
            src, dst = mine.at[p], far.at[p, pl.ds(0, 1 + near)]
        elif relayed:
            src, dst = far.at[p, near + 2], far.at[p, near + level]
        else:
            src, dst = mine.at[p, 0], far.at[p, near + level]
        return pltpu.make_async_remote_copy(
            src_ref=src,
            dst_ref=dst,
            send_sem=send_sem.at[p, kind],
            recv_sem=recv_sem.at[p, level],
            device_id={"tm": there, "head": side},
            device_id_type=MESH,
        )

    direct = [(1, 2, me + 4, me + 4 < blocks), (0, 0, me + 1, me + 1 < blocks)]
    later = []
    if relay:
        low = lax.rem(me, 4) < 2
        alone = me + 4 >= blocks
        direct.append((2, 1, me + 2, jnp.logical_and(me + 2 < blocks, jnp.logical_or(low, alone))))
        later.append((3, 3, me + 4, jnp.logical_and(me >= 4, me + 4 < blocks)))
        later.append((4, 1, me - 2, jnp.logical_and(me >= 4, jnp.logical_not(low))))
    else:
        direct.append((2, 1, me + 2, me + 2 < blocks))
    for l in range(3, depth):
        if not (relay and l == 3):
            direct.append((2 + l, l, me + 2**l, me + 2**l < blocks))

    def send_far(p):
        for kind, level, there, when in direct:

            @pl.when(when)
            def _():
                far_copy(p, kind, level, there, False).start()

    send_far(0)
    lax.fori_loop(0, steps - 1, project, 0)

    for l in range(depth):
        slots = range(1 + near) if l == 0 else [near + l]
        valid = jnp.where(me >= 2**l, 1.0, 0.0).astype(jnp.bfloat16)
        for b in slots:
            ones_s[:, b * PK : (b + 1) * PK] = jnp.broadcast_to(valid, (ONES, PK))

        @pl.when(me < 2**l)
        def _():
            for p in range(pairs):
                for b in slots:
                    far[p, b, :PK, :] = jnp.broadcast_to(k_s[p, 0:1, :], (PK, PAIR))
                    far[p, b, PK:, :] = jnp.zeros((PK, PAIR), jnp.bfloat16)

    def arrived(p, level):
        @pl.when(me >= 2**level)
        def _():
            far_copy(p, 0, level, me, False).wait_recv()

    def pass_on(p):
        arrived(p, 2)
        for kind, level, there, when in later:

            @pl.when(when)
            def _():
                far_copy(p, kind, level, there, True).start()

    pass_on(0)
    if pairs > 1:
        send_far(1)

    first = lax.broadcasted_iota(jnp.int32, (1, PAIR), 1) < DH

    def query(p, h, c):
        rows = pl.ds(c * chunk if isinstance(c, int) else pl.multiple_of(c * chunk, chunk), chunk)
        q = q_s[p, rows, :]
        keep = jnp.broadcast_to(first == (h == 0), q.shape)
        q = jnp.where(keep, q, jnp.zeros_like(q))
        return q if exact else jnp.concatenate([q, shift_s[rows, :]], 1)

    lane = lax.broadcasted_iota(jnp.int32, (1, PAIR), 1)

    def key(k, p, h):
        if exact:
            return k
        pick = jnp.where(lane == 2 * p + h, 1.0, 0.0).astype(jnp.bfloat16)
        return jnp.concatenate([k, jnp.broadcast_to(pick, k.shape)], 1)

    def fold(s, v, state):
        if exact:
            return attend(s, v, state)
        acc = jnp.dot(v, jnp.exp2(s).astype(jnp.bfloat16), preferred_element_type=jnp.float32)
        return (acc,) if state is None else (state[0] + acc,)

    def ones(columns):
        return jnp.ones((ONES, columns), jnp.bfloat16)

    causal = lax.broadcasted_iota(jnp.int32, (DIAG, DIAG), 0) <= lax.broadcasted_iota(
        jnp.int32, (DIAG, DIAG), 1
    )

    def local(p, h):
        vrows = pl.ds(pl.multiple_of(p * PAIR + h * DH, DH), DH)
        for c in range(chunks):
            q = query(p, h, c)
            for t in range(0, chunk, DIAG):
                state = None
                end = c * chunk + t + DIAG
                for at in range(0, end, SPAN):
                    count = min(SPAN, end - at)
                    s = scores(key(k_s[p, at : at + count, :], p, h), q[t : t + DIAG])
                    v = jnp.concatenate([vt_s[vrows, at : at + count], ones(count)], 0)
                    if at + count == end:
                        corner = jnp.where(causal, s[count - DIAG :], NEG)
                        s = jnp.concatenate([s[: count - DIAG], corner], 0) if count > DIAG else corner
                    state = fold(s, v, state)
                acc_s[h, c, :, t : t + DIAG] = state[-1]
                if exact:
                    top_s[h, c, :, t : t + DIAG] = jnp.broadcast_to(state[0], (8, DIAG))

    total = near + depth

    def distant(p, h, c):
        q = query(p, h, c)
        held = h
        state = (top_s[held, c, 0:1, :], acc_s[held, c]) if exact else (acc_s[held, c],)
        for b in range(0, total, GROUP):
            group = range(b, min(b + GROUP, total))
            k = jnp.concatenate([far[p, g, :PK, :] for g in group], 0)
            s = scores(key(k, p, h), q)
            v = jnp.concatenate(
                [
                    far[p, g, pl.ds(pl.multiple_of(PK + half * PAIR + h * DH, DH), DH), :]
                    for g in group
                    for half in range(2)
                ],
                1,
            )
            v = jnp.concatenate([v, ones_s[:, b * PK : b * PK + len(group) * PK]], 0)
            state = fold(s, v, state)
        acc = state[-1]
        rows = pl.ds(pl.multiple_of(h * DH, DH), DH)
        ctx[side, p, c, rows, :] = (acc[:DH] / acc[DH : DH + 1]).astype(jnp.bfloat16)

    def check():
        longest = jnp.sqrt(jnp.maximum(flag_s[depth - 1, 0:1], flag_r[depth - 1, 0:1])) * 1.01
        bound = jnp.sqrt(norm_s[...]) * 1.01 * longest
        over = jnp.maximum(bound + shift_s[...].astype(jnp.float32) - ROOM, bound - LARGE)
        flag_s[depth] = jnp.broadcast_to(jnp.max(over, axis=0, keepdims=True), flag_s.shape[1:])

    def tell(r):
        d = 2 ** (r % depth)
        there = me + d * (1 - 2 * lax.rem(me // d, 2))
        return pltpu.make_async_remote_copy(
            src_ref=flag_s.at[r],
            dst_ref=flag_r.at[r],
            send_sem=fsend_sem.at[r],
            recv_sem=frecv_sem.at[r],
            device_id={"tm": there, "head": side},
            device_id_type=MESH,
        )

    def heard(r):
        tell(r).wait()
        if r == depth - 1:
            check()
        else:
            flag_s[r + 1] = jnp.maximum(flag_s[r], flag_r[r])

    def spread(r):
        if r == 0:
            flag_s[0] = kmax_s[...]
        else:
            heard(r - 1)
        tell(r).start()

    def tell_side(s):
        return pltpu.make_async_remote_copy(
            src_ref=flag_s.at[2 * depth],
            dst_ref=flag_x.at[s - 1],
            send_sem=fsend_sem.at[2 * depth + s - 1],
            recv_sem=frecv_sem.at[2 * depth + s - 1],
            device_id={"tm": me, "head": lax.rem(side + s, sides)},
            device_id_type=MESH,
        )

    def cross(p, c, h, s):
        rows = pl.ds(pl.multiple_of(h * DH, DH), DH)
        return pltpu.make_async_remote_copy(
            src_ref=ctx.at[side, p, c, rows],
            dst_ref=ctx.at[side, p, c, rows],
            send_sem=xsend_sem.at[p, 2 * c + h, s - 1],
            recv_sem=xrecv_sem.at[p, 2 * c + h, s - 1],
            device_id={"tm": me, "head": lax.rem(side + s, sides)},
            device_id_type=MESH,
        )

    def crossed(p, c, h, s):
        rows = pl.ds(pl.multiple_of(h * DH, DH), DH)
        there = lax.rem(side + sides - s, sides)
        return pltpu.make_async_remote_copy(
            src_ref=ctx.at[there, p, c, rows],
            dst_ref=ctx.at[there, p, c, rows],
            send_sem=xsend_sem.at[p, 2 * c + h, s - 1],
            recv_sem=xrecv_sem.at[p, 2 * c + h, s - 1],
            device_id={"tm": me, "head": there},
            device_id_type=MESH,
        )

    turns = 2 * pairs
    rounds = 2 * depth

    def step(p, carry):
        def own(h, carry):
            if not exact:
                for r in range(min(rounds, turns)):

                    @pl.when(2 * p + h == r)
                    def _():
                        spread(r)

            local(p, h)
            return carry

        lax.fori_loop(0, 2, own, 0)

        for l in range(depth):
            if l != 2:
                arrived(p, l)

        @pl.when(p + 1 < pairs)
        def _():
            pass_on(p + 1)

        @pl.when(p + 2 < pairs)
        def _():
            send_far(p + 2)

        def part(c, carry):
            def head(h, carry):
                distant(p, h, c)
                for s in range(1, sides):
                    cross(p, c, h, s).start()
                return carry

            lax.fori_loop(0, 2, head, 0)
            return carry

        lax.fori_loop(0, chunks, part, 0)
        return carry

    lax.fori_loop(0, pairs, step, 0)
    load_out.wait()
    if not exact:
        for r in range(turns, rounds):
            spread(r)
        heard(rounds - 1)
        for x in range(1, sides):
            tell_side(x).start()

    def finish(c, carry):
        def product(x):
            weights = wout_s[pl.ds(pl.multiple_of(x * width, width), width), :]
            context = ctx[x, :, c].reshape(width, chunk)
            return lax.dot_general(context, weights, TN, preferred_element_type=jnp.float32)

        total = product(side)
        for s in range(1, sides):

            def here(n, carry):
                crossed(n // 2, c, lax.rem(n, 2), s).wait_recv()
                return carry

            lax.fori_loop(0, 2 * pairs, here, 0)
            total = total + product(lax.rem(side + sides - s, sides))
        out_ref[pl.ds(pl.multiple_of(c * chunk, chunk), chunk), :] = total.astype(jnp.bfloat16)
        return carry

    lax.fori_loop(0, chunks, finish, 0)
    if exact:
        flag_ref[...] = jnp.zeros_like(flag_ref)
    else:
        worst = flag_s[2 * depth]
        for x in range(1, sides):
            tell_side(x).wait()
            worst = jnp.maximum(worst, flag_x[x - 1])
        flag_ref[...] = jnp.broadcast_to(jnp.max(worst, axis=1, keepdims=True), flag_ref.shape)

    def settle(p, carry):
        for kind, level, there, when in direct + later:

            @pl.when(when)
            def _():
                far_copy(p, kind, level, there, (kind, level, there, when) in later).wait_send()

        def part(n, carry):
            for s in range(1, sides):
                cross(p, n // 2, lax.rem(n, 2), s).wait_send()
            return carry

        lax.fori_loop(0, 2 * chunks, part, 0)
        return carry

    lax.fori_loop(0, pairs, settle, 0)


def run(exact, frames, w_query, w_key, w_value, w_out):
    block, model = frames.shape
    width = w_query.shape[1]
    pairs = width // PAIR
    blocks = lax.axis_size("tm")
    sides = lax.axis_size("head")
    depth = 0
    while 2**depth < blocks:
        depth = depth + 1
    near = WIN // PK
    chunk = min(CHUNK, block)
    chunks = block // chunk
    others = max(1, sides - 1)
    bf16, f32 = jnp.bfloat16, jnp.float32
    anywhere = pl.BlockSpec(memory_space=pl.ANY)
    vmem = pl.BlockSpec(memory_space=pltpu.VMEM)
    scored = block * block // 2 + block * PK * (near + depth)
    blob = 2 * PK
    return pl.pallas_call(
        functools.partial(kernel, exact, blocks, sides, depth),
        out_shape=[
            jax.ShapeDtypeStruct((block, width), bf16),
            jax.ShapeDtypeStruct((8, PAIR), f32),
        ],
        in_specs=[anywhere] * 5,
        out_specs=[vmem, vmem],
        scratch_shapes=[
            pltpu.VMEM((block, model), bf16),
            pltpu.VMEM((model, width), bf16),
            pltpu.VMEM((model, width), bf16),
            pltpu.VMEM((model, width), bf16),
            pltpu.VMEM((pairs, block, PAIR), bf16),
            pltpu.VMEM((pairs, block, PAIR), bf16),
            pltpu.VMEM((width, block), bf16),
            pltpu.VMEM((width, model), bf16),
            pltpu.VMEM((PK, model), bf16),
            pltpu.VMEM((block, PAIR), bf16),
            pltpu.VMEM((block, PAIR), f32),
            pltpu.VMEM((8, PAIR), f32),
            pltpu.VMEM((2 * depth + 1, 8, PAIR), f32),
            pltpu.VMEM((2 * depth, 8, PAIR), f32),
            pltpu.VMEM((others, 8, PAIR), f32),
            pltpu.VMEM((pairs, 1 + near, blob, PAIR), bf16),
            pltpu.VMEM((pairs, near + depth, blob, PAIR), bf16),
            pltpu.VMEM((ONES, (near + depth) * PK), bf16),
            pltpu.VMEM((2, chunks, DH + ONES, chunk), f32),
            pltpu.VMEM((2, chunks, 8, chunk), f32),
            pltpu.VMEM((sides, pairs, chunks, PAIR, chunk), bf16),
            pltpu.VMEM((model, width), bf16),
            pltpu.SemaphoreType.DMA,
            pltpu.SemaphoreType.DMA((3 + block // ROWS,)),
            pltpu.SemaphoreType.DMA((2 * depth + others,)),
            pltpu.SemaphoreType.DMA((2 * depth + others,)),
            pltpu.SemaphoreType.DMA((pairs, 3 + depth)),
            pltpu.SemaphoreType.DMA((pairs, depth)),
            pltpu.SemaphoreType.DMA((pairs, 2 * chunks, others)),
            pltpu.SemaphoreType.DMA((pairs, 2 * chunks, others)),
        ],
        compiler_params=pltpu.CompilerParams(
            collective_id=int(exact), has_side_effects=True, vmem_limit_bytes=58 * 2**20
        ),
        cost_estimate=pl.CostEstimate(
            flops=8 * width * model * block + 4 * width * scored,
            bytes_accessed=4 * block * model,
            transcendentals=0,
        ),
    )(frames, w_query, w_key, w_value, w_out)


def body(*args):
    out, over = run(False, *args)
    return lax.cond(over[0, 0] > 0, lambda: run(True, *args)[0], lambda: out)


def solution(mesh):
    in_specs = (P("tm", None), P(None, "head"), P(None, "head"), P(None, "head"), P())
    out_specs = P("tm", "head")
    return jax.shard_map(body, mesh=mesh, in_specs=in_specs, out_specs=out_specs, check_vma=False)
```

```python
import functools
import math

import jax
import jax.numpy as jnp
from jax import lax
from jax.experimental import pallas as pl
from jax.experimental.pallas import tpu as pltpu
from jax.sharding import PartitionSpec as P

DH = 64
PAIR = 2 * DH
WIN = 512
PK = 256
CHUNK = 1024
DIAG = 512
SPAN = 2048
ROWS = 512
ONES = 16
NEG = -1e30
ABOVE = 90.0
ROOM = 100.0
LARGE = 2000.0
GROUP = 3
NT = (((1,), (1,)), ((), ()))
TN = (((0,), (0,)), ((), ()))
MESH = pl.DeviceIdType.MESH


def scores(k, q):
    return lax.dot_general(k, q, NT, preferred_element_type=jnp.float32)


def attend(s, v, state):
    new = jnp.max(s, axis=0, keepdims=True)
    if state is not None:
        new = jnp.maximum(state[0], new)
    p = jnp.exp2(s - new).astype(jnp.bfloat16)
    acc = jnp.dot(v, p, preferred_element_type=jnp.float32)
    if state is not None:
        acc = acc + state[1] * jnp.exp2(state[0] - new)
    return new, acc


def kernel(
    exact,
    blocks,
    sides,
    depth,
    frames_in,
    wq_in,
    wk_in,
    wv_in,
    wout_ref,
    out_ref,
    flag_ref,
    frames_ref,
    wq_ref,
    wk_ref,
    wv_ref,
    q_s,
    k_s,
    vt_s,
    wvt_s,
    pooled_s,
    shift_s,
    norm_s,
    kmax_s,
    flag_s,
    flag_r,
    flag_x,
    mine,
    far,
    ones_s,
    acc_s,
    top_s,
    ctx,
    wout_s,
    wout_sem,
    in_sem,
    fsend_sem,
    frecv_sem,
    send_sem,
    recv_sem,
    xsend_sem,
    xrecv_sem,
):
    me = lax.axis_index("tm")
    side = lax.axis_index("head")
    block = frames_ref.shape[0]
    width = wq_ref.shape[1]
    pairs = width // PAIR
    chunk = min(CHUNK, block)
    chunks = block // chunk
    near = WIN // PK
    relay = blocks > 8

    load_out = pltpu.make_async_copy(
        wout_ref.at[:, pl.ds(pl.multiple_of(side * width, width), width)], wout_s, wout_sem
    )

    steps = block // ROWS

    def load(i):
        if i < 3:
            refs = [(wk_in, wk_ref), (wq_in, wq_ref), (wv_in, wv_ref)]
            return pltpu.make_async_copy(*refs[i], in_sem.at[i])

    def load_rows(i):
        rows = pl.ds(pl.multiple_of(i * ROWS, ROWS), ROWS)
        return pltpu.make_async_copy(frames_in.at[rows], frames_ref.at[rows], in_sem.at[3 + i])

    load(2).start()
    load(0).start()
    load_rows(steps - 1).start()
    load(1).start()
    for i in range(steps - 1):
        load_rows(i).start()
    load_out.start()

    barrier = pltpu.get_barrier_semaphore()
    reach = [2**l for l in range(depth)]
    count = sides - 1
    for d in reach:
        for there in (me + d, me - d):
            inside = jnp.logical_and(there >= 0, there < blocks)
            count = count + inside.astype(jnp.int32)

            @pl.when(inside)
            def _():
                pl.semaphore_signal(
                    barrier, inc=1, device_id={"tm": there, "head": side}, device_id_type=MESH
                )

    for s in range(1, sides):
        pl.semaphore_signal(
            barrier,
            inc=1,
            device_id={"tm": me, "head": lax.rem(side + s, sides)},
            device_id_type=MESH,
        )

    span = block // PK
    slots_in = ROWS // span
    slot = lax.broadcasted_iota(jnp.int32, (slots_in, ROWS), 0) * span
    frame = lax.broadcasted_iota(jnp.int32, (slots_in, ROWS), 1)
    pool = jnp.where(
        jnp.logical_and(frame >= slot, frame < slot + span), 1.0 / span, 0.0
    ).astype(jnp.bfloat16)
    column = lax.broadcasted_iota(jnp.int32, (width, PAIR), 0)
    owner = lax.broadcasted_iota(jnp.int32, (width, PAIR), 1) * DH
    by_head = jnp.where(
        jnp.logical_and(column >= owner, column < owner + DH), 1.0, 0.0
    ).astype(jnp.bfloat16)
    factor = DH**-0.5 * math.log2(math.e)
    kmax_s[...] = jnp.zeros_like(kmax_s)
    load(2).wait()
    wvt_s[...] = wv_ref[...].T
    load(0).wait()
    load_rows(steps - 1).wait()
    load(1).wait()

    def heads(x):
        return jnp.dot(x.astype(jnp.bfloat16), by_head, preferred_element_type=jnp.float32)

    def project(i, carry):
        rows = pl.ds(pl.multiple_of(i * ROWS, ROWS), ROWS)
        f = frames_ref[rows, :]
        kf = jnp.dot(f, wk_ref[...], preferred_element_type=jnp.float32)
        qf = jnp.dot(f, wq_ref[...], preferred_element_type=jnp.float32) * factor
        k, q = kf.astype(jnp.bfloat16), qf.astype(jnp.bfloat16)
        for p in range(pairs):
            k_s[p, rows, :] = k[:, p * PAIR : (p + 1) * PAIR]
            q_s[p, rows, :] = q[:, p * PAIR : (p + 1) * PAIR]
        if not exact:
            longest = jnp.max(heads(kf * kf), axis=0, keepdims=True)
            kmax_s[...] = jnp.maximum(kmax_s[...], jnp.broadcast_to(longest, kmax_s.shape))
            norm_s[rows, :] = heads(qf * qf)
            shift_s[rows, :] = (-ABOVE - heads(qf * kf)).astype(jnp.bfloat16)
        v = scores(wvt_s[...], f).astype(jnp.bfloat16)
        vt_s[:, rows] = v
        return carry

    project(steps - 1, 0)
    for i in range(steps):
        if i < steps - 1:
            load_rows(i).wait()
        pooled_s[i * slots_in : (i + 1) * slots_in, :] = jnp.dot(
            pool, frames_ref[i * ROWS : (i + 1) * ROWS, :], preferred_element_type=jnp.float32
        ).astype(jnp.bfloat16)
    pooled_k = jnp.dot(pooled_s[...], wk_ref[...], preferred_element_type=jnp.float32)
    pooled_k = pooled_k.astype(jnp.bfloat16)
    pooled_v = scores(wvt_s[...], pooled_s[...]).astype(jnp.bfloat16)
    for p in range(pairs):
        mine[p, 0, :PK, :] = pooled_k[:, p * PAIR : (p + 1) * PAIR]
        for half in range(2):
            mine[p, 0, PK + half * PAIR : PK + (half + 1) * PAIR, :] = pooled_v[
                p * PAIR : (p + 1) * PAIR, half * PAIR : (half + 1) * PAIR
            ]
        for j in range(near):
            at = block - WIN + j * PK
            mine[p, 1 + j, :PK, :] = k_s[p, at : at + PK, :]
            for half in range(2):
                first = at + half * PAIR
                mine[p, 1 + j, PK + half * PAIR : PK + (half + 1) * PAIR, :] = vt_s[
                    p * PAIR : (p + 1) * PAIR, first : first + PAIR
                ]

    pl.semaphore_wait(barrier, count)

    def far_copy(p, kind, level, there, relayed):
        if level == 0:
            src, dst = mine.at[p], far.at[p, pl.ds(0, 1 + near)]
        elif relayed:
            src, dst = far.at[p, near + 2], far.at[p, near + level]
        else:
            src, dst = mine.at[p, 0], far.at[p, near + level]
        return pltpu.make_async_remote_copy(
            src_ref=src,
            dst_ref=dst,
            send_sem=send_sem.at[p, kind],
            recv_sem=recv_sem.at[p, level],
            device_id={"tm": there, "head": side},
            device_id_type=MESH,
        )

    direct = [(1, 2, me + 4, me + 4 < blocks), (0, 0, me + 1, me + 1 < blocks)]
    later = []
    if relay:
        low = lax.rem(me, 4) < 2
        alone = me + 4 >= blocks
        direct.insert(1, (2, 1, me + 2, jnp.logical_and(me + 2 < blocks, jnp.logical_or(low, alone))))
        later.append((3, 3, me + 4, jnp.logical_and(me >= 4, me + 4 < blocks)))
        later.append((4, 1, me - 2, jnp.logical_and(me >= 4, jnp.logical_not(low))))
    else:
        direct.insert(1, (2, 1, me + 2, me + 2 < blocks))
    for l in range(3, depth):
        if not (relay and l == 3):
            direct.append((2 + l, l, me + 2**l, me + 2**l < blocks))

    def send_far(p):
        for kind, level, there, when in direct:

            @pl.when(when)
            def _():
                far_copy(p, kind, level, there, False).start()

    send_far(0)
    lax.fori_loop(0, steps - 1, project, 0)

    for l in range(depth):
        slots = range(1 + near) if l == 0 else [near + l]
        valid = jnp.where(me >= 2**l, 1.0, 0.0).astype(jnp.bfloat16)
        for b in slots:
            ones_s[:, b * PK : (b + 1) * PK] = jnp.broadcast_to(valid, (ONES, PK))

        @pl.when(me < 2**l)
        def _():
            for p in range(pairs):
                for b in slots:
                    far[p, b, :PK, :] = jnp.broadcast_to(k_s[p, 0:1, :], (PK, PAIR))
                    far[p, b, PK:, :] = jnp.zeros((PK, PAIR), jnp.bfloat16)

    def arrived(p, level):
        @pl.when(me >= 2**level)
        def _():
            far_copy(p, 0, level, me, False).wait_recv()

    def pass_on(p):
        arrived(p, 2)
        for kind, level, there, when in later:

            @pl.when(when)
            def _():
                far_copy(p, kind, level, there, True).start()

    pass_on(0)
    if pairs > 1:
        send_far(1)

    first = lax.broadcasted_iota(jnp.int32, (1, PAIR), 1) < DH

    def query(p, h, c):
        rows = pl.ds(c * chunk if isinstance(c, int) else pl.multiple_of(c * chunk, chunk), chunk)
        q = q_s[p, rows, :]
        keep = jnp.broadcast_to(first == (h == 0), q.shape)
        q = jnp.where(keep, q, jnp.zeros_like(q))
        return q if exact else jnp.concatenate([q, shift_s[rows, :]], 1)

    lane = lax.broadcasted_iota(jnp.int32, (1, PAIR), 1)

    def key(k, p, h):
        if exact:
            return k
        pick = jnp.where(lane == 2 * p + h, 1.0, 0.0).astype(jnp.bfloat16)
        return jnp.concatenate([k, jnp.broadcast_to(pick, k.shape)], 1)

    def fold(s, v, state):
        if exact:
            return attend(s, v, state)
        acc = jnp.dot(v, jnp.exp2(s).astype(jnp.bfloat16), preferred_element_type=jnp.float32)
        return (acc,) if state is None else (state[0] + acc,)

    def ones(columns):
        return jnp.ones((ONES, columns), jnp.bfloat16)

    causal = lax.broadcasted_iota(jnp.int32, (DIAG, DIAG), 0) <= lax.broadcasted_iota(
        jnp.int32, (DIAG, DIAG), 1
    )

    def local(p, h):
        vrows = pl.ds(pl.multiple_of(p * PAIR + h * DH, DH), DH)
        for c in range(chunks):
            q = query(p, h, c)
            for t in range(0, chunk, DIAG):
                state = None
                end = c * chunk + t + DIAG
                for at in range(0, end, SPAN):
                    count = min(SPAN, end - at)
                    s = scores(key(k_s[p, at : at + count, :], p, h), q[t : t + DIAG])
                    v = jnp.concatenate([vt_s[vrows, at : at + count], ones(count)], 0)
                    if at + count == end:
                        corner = jnp.where(causal, s[count - DIAG :], NEG)
                        s = jnp.concatenate([s[: count - DIAG], corner], 0) if count > DIAG else corner
                    state = fold(s, v, state)
                acc_s[h, c, :, t : t + DIAG] = state[-1]
                if exact:
                    top_s[h, c, :, t : t + DIAG] = jnp.broadcast_to(state[0], (8, DIAG))

    total = near + depth

    def distant(p, h, c):
        q = query(p, h, c)
        held = h
        state = (top_s[held, c, 0:1, :], acc_s[held, c]) if exact else (acc_s[held, c],)
        for b in range(0, total, GROUP):
            group = range(b, min(b + GROUP, total))
            k = jnp.concatenate([far[p, g, :PK, :] for g in group], 0)
            s = scores(key(k, p, h), q)
            v = jnp.concatenate(
                [
                    far[p, g, pl.ds(pl.multiple_of(PK + half * PAIR + h * DH, DH), DH), :]
                    for g in group
                    for half in range(2)
                ],
                1,
            )
            v = jnp.concatenate([v, ones_s[:, b * PK : b * PK + len(group) * PK]], 0)
            state = fold(s, v, state)
        acc = state[-1]
        rows = pl.ds(pl.multiple_of(h * DH, DH), DH)
        ctx[side, p, c, rows, :] = (acc[:DH] / acc[DH : DH + 1]).astype(jnp.bfloat16)

    def check():
        longest = jnp.sqrt(jnp.maximum(flag_s[depth - 1, 0:1], flag_r[depth - 1, 0:1])) * 1.01
        bound = jnp.sqrt(norm_s[...]) * 1.01 * longest
        over = jnp.maximum(bound + shift_s[...].astype(jnp.float32) - ROOM, bound - LARGE)
        flag_s[depth] = jnp.broadcast_to(jnp.max(over, axis=0, keepdims=True), flag_s.shape[1:])

    def tell(r):
        d = 2 ** (r % depth)
        there = me + d * (1 - 2 * lax.rem(me // d, 2))
        return pltpu.make_async_remote_copy(
            src_ref=flag_s.at[r],
            dst_ref=flag_r.at[r],
            send_sem=fsend_sem.at[r],
            recv_sem=frecv_sem.at[r],
            device_id={"tm": there, "head": side},
            device_id_type=MESH,
        )

    def heard(r):
        tell(r).wait()
        if r == depth - 1:
            check()
        else:
            flag_s[r + 1] = jnp.maximum(flag_s[r], flag_r[r])

    def spread(r):
        if r == 0:
            flag_s[0] = kmax_s[...]
        else:
            heard(r - 1)
        tell(r).start()

    def tell_side(s):
        return pltpu.make_async_remote_copy(
            src_ref=flag_s.at[2 * depth],
            dst_ref=flag_x.at[s - 1],
            send_sem=fsend_sem.at[2 * depth + s - 1],
            recv_sem=frecv_sem.at[2 * depth + s - 1],
            device_id={"tm": me, "head": lax.rem(side + s, sides)},
            device_id_type=MESH,
        )

    def cross(p, c, h, s):
        rows = pl.ds(pl.multiple_of(h * DH, DH), DH)
        return pltpu.make_async_remote_copy(
            src_ref=ctx.at[side, p, c, rows],
            dst_ref=ctx.at[side, p, c, rows],
            send_sem=xsend_sem.at[p, 2 * c + h, s - 1],
            recv_sem=xrecv_sem.at[p, 2 * c + h, s - 1],
            device_id={"tm": me, "head": lax.rem(side + s, sides)},
            device_id_type=MESH,
        )

    def crossed(p, c, h, s):
        rows = pl.ds(pl.multiple_of(h * DH, DH), DH)
        there = lax.rem(side + sides - s, sides)
        return pltpu.make_async_remote_copy(
            src_ref=ctx.at[there, p, c, rows],
            dst_ref=ctx.at[there, p, c, rows],
            send_sem=xsend_sem.at[p, 2 * c + h, s - 1],
            recv_sem=xrecv_sem.at[p, 2 * c + h, s - 1],
            device_id={"tm": me, "head": there},
            device_id_type=MESH,
        )

    turns = 2 * pairs
    rounds = 2 * depth

    def step(p, carry):
        def own(h, carry):
            if not exact:
                for r in range(min(rounds, turns)):

                    @pl.when(2 * p + h == r)
                    def _():
                        spread(r)

            local(p, h)
            return carry

        lax.fori_loop(0, 2, own, 0)

        for l in range(depth):
            if l != 2:
                arrived(p, l)

        @pl.when(p + 1 < pairs)
        def _():
            pass_on(p + 1)

        @pl.when(p + 2 < pairs)
        def _():
            send_far(p + 2)

        def part(c, carry):
            def head(h, carry):
                distant(p, h, c)
                for s in range(1, sides):
                    cross(p, c, h, s).start()
                return carry

            lax.fori_loop(0, 2, head, 0)
            return carry

        lax.fori_loop(0, chunks, part, 0)
        return carry

    lax.fori_loop(0, pairs, step, 0)
    load_out.wait()
    if not exact:
        for r in range(turns, rounds):
            spread(r)
        heard(rounds - 1)
        for x in range(1, sides):
            tell_side(x).start()

    def finish(c, carry):
        def product(x):
            weights = wout_s[pl.ds(pl.multiple_of(x * width, width), width), :]
            context = ctx[x, :, c].reshape(width, chunk)
            return lax.dot_general(context, weights, TN, preferred_element_type=jnp.float32)

        total = product(side)
        for s in range(1, sides):

            def here(n, carry):
                crossed(n // 2, c, lax.rem(n, 2), s).wait_recv()
                return carry

            lax.fori_loop(0, 2 * pairs, here, 0)
            total = total + product(lax.rem(side + sides - s, sides))
        out_ref[pl.ds(pl.multiple_of(c * chunk, chunk), chunk), :] = total.astype(jnp.bfloat16)
        return carry

    lax.fori_loop(0, chunks, finish, 0)
    if exact:
        flag_ref[...] = jnp.zeros_like(flag_ref)
    else:
        worst = flag_s[2 * depth]
        for x in range(1, sides):
            tell_side(x).wait()
            worst = jnp.maximum(worst, flag_x[x - 1])
        flag_ref[...] = jnp.broadcast_to(jnp.max(worst, axis=1, keepdims=True), flag_ref.shape)

    def settle(p, carry):
        for kind, level, there, when in direct + later:

            @pl.when(when)
            def _():
                far_copy(p, kind, level, there, (kind, level, there, when) in later).wait_send()

        def part(n, carry):
            for s in range(1, sides):
                cross(p, n // 2, lax.rem(n, 2), s).wait_send()
            return carry

        lax.fori_loop(0, 2 * chunks, part, 0)
        return carry

    lax.fori_loop(0, pairs, settle, 0)


def run(exact, frames, w_query, w_key, w_value, w_out):
    block, model = frames.shape
    width = w_query.shape[1]
    pairs = width // PAIR
    blocks = lax.axis_size("tm")
    sides = lax.axis_size("head")
    depth = 0
    while 2**depth < blocks:
        depth = depth + 1
    near = WIN // PK
    chunk = min(CHUNK, block)
    chunks = block // chunk
    others = max(1, sides - 1)
    bf16, f32 = jnp.bfloat16, jnp.float32
    anywhere = pl.BlockSpec(memory_space=pl.ANY)
    vmem = pl.BlockSpec(memory_space=pltpu.VMEM)
    scored = block * block // 2 + block * PK * (near + depth)
    blob = 2 * PK
    return pl.pallas_call(
        functools.partial(kernel, exact, blocks, sides, depth),
        out_shape=[
            jax.ShapeDtypeStruct((block, width), bf16),
            jax.ShapeDtypeStruct((8, PAIR), f32),
        ],
        in_specs=[anywhere] * 5,
        out_specs=[vmem, vmem],
        scratch_shapes=[
            pltpu.VMEM((block, model), bf16),
            pltpu.VMEM((model, width), bf16),
            pltpu.VMEM((model, width), bf16),
            pltpu.VMEM((model, width), bf16),
            pltpu.VMEM((pairs, block, PAIR), bf16),
            pltpu.VMEM((pairs, block, PAIR), bf16),
            pltpu.VMEM((width, block), bf16),
            pltpu.VMEM((width, model), bf16),
            pltpu.VMEM((PK, model), bf16),
            pltpu.VMEM((block, PAIR), bf16),
            pltpu.VMEM((block, PAIR), f32),
            pltpu.VMEM((8, PAIR), f32),
            pltpu.VMEM((2 * depth + 1, 8, PAIR), f32),
            pltpu.VMEM((2 * depth, 8, PAIR), f32),
            pltpu.VMEM((others, 8, PAIR), f32),
            pltpu.VMEM((pairs, 1 + near, blob, PAIR), bf16),
            pltpu.VMEM((pairs, near + depth, blob, PAIR), bf16),
            pltpu.VMEM((ONES, (near + depth) * PK), bf16),
            pltpu.VMEM((2, chunks, DH + ONES, chunk), f32),
            pltpu.VMEM((2, chunks, 8, chunk), f32),
            pltpu.VMEM((sides, pairs, chunks, PAIR, chunk), bf16),
            pltpu.VMEM((model, width), bf16),
            pltpu.SemaphoreType.DMA,
            pltpu.SemaphoreType.DMA((3 + block // ROWS,)),
            pltpu.SemaphoreType.DMA((2 * depth + others,)),
            pltpu.SemaphoreType.DMA((2 * depth + others,)),
            pltpu.SemaphoreType.DMA((pairs, 3 + depth)),
            pltpu.SemaphoreType.DMA((pairs, depth)),
            pltpu.SemaphoreType.DMA((pairs, 2 * chunks, others)),
            pltpu.SemaphoreType.DMA((pairs, 2 * chunks, others)),
        ],
        compiler_params=pltpu.CompilerParams(
            collective_id=int(exact), has_side_effects=True, vmem_limit_bytes=58 * 2**20
        ),
        cost_estimate=pl.CostEstimate(
            flops=8 * width * model * block + 4 * width * scored,
            bytes_accessed=4 * block * model,
            transcendentals=0,
        ),
    )(frames, w_query, w_key, w_value, w_out)


def body(*args):
    out, over = run(False, *args)
    return lax.cond(over[0, 0] > 0, lambda: run(True, *args)[0], lambda: out)


def solution(mesh):
    in_specs = (P("tm", None), P(None, "head"), P(None, "head"), P(None, "head"), P())
    out_specs = P("tm", "head")
    return jax.shard_map(body, mesh=mesh, in_specs=in_specs, out_specs=out_specs, check_vma=False)
```
